128 devices in a mesh: grp: 8 (over x, core), wide: 16 (over z, y).
Axes of the slice: x: 4, y: 4, z: 4, core: 2. Of those that a mesh axis runs over, the one named last changes fastest.
Arguments:
- amplitudes: float32 [4096, 64, 512], P(('grp', 'wide')), may hold values from -6 to 6
- integrals: float32 [8, 512, 512], P('grp'), may hold values from -0.25 to 0.25
- base_residual: float32 [128, 64, 512], P(('grp', 'wide')), may hold values from -6 to 6
- occ_gap: float32 [128, 64], P(('grp', 'wide')), may hold values from 0.5 to 4
- virt_sum: float32 [512], replicated, may hold values from 0.5 to 4
- task_amp: int32 [128, 96], P(('grp', 'wide')), may hold values from 0 to 511, as said below
- task_int: int32 [128, 96], P(('grp', 'wide')), may hold values from 0 to 7
- task_res: int32 [128, 96], P(('grp', 'wide')), may hold values from 0 to 15, as said below
- task_count: int32 [128], P(('grp', 'wide')), may hold values from 6 to 96, as said below
- res_owner: int32 [8, 16], P('grp'), may hold values from 0 to 15, as said below
- amp_label: int32 [4096], P(('grp', 'wide')), may hold values from 0 to 3
- int_label: int32 [8], replicated, may hold values from 0 to 3
Outputs:
- doubles_residual: float32 [128, 64, 512], P(('grp', 'wide'))
The draws below stay inside these ranges and needn't reach their ends.
Inputs may be any that keep to these rules, and one draw needn't show every extreme that they name: `task_amp`: amplitude block t of a grp row is kept by the device of wide index t // 32 of that row, at its local position t % 32. Among the used slots of one device at most 6 name blocks kept by one device. `task_res`: among the used slots of one device at most 6 name tiles whose position (see res_owner) lies on one device. Slots from task_count on are unused; their entries are arbitrary values within the stated ranges. `res_owner`: each row is a permutation; position p of a grp row lies on the device of wide index p, at its local position p % 1.
All inputs are finite; a program needn't handle non-finite values.
Results may differ from the reference program's by a relative error of at most 0.0001.
Values sent between devices are 32-bit elements; how exact they have to be, the bound alone decides.
A program may use at most 128 MiB of HBM per device.

```python
import jax
import jax.numpy as jnp
from jax import lax

TILE_ROWS = 64
BLOCK_COLS = 512
WINDOW = 512
TASK_SLOTS = 96
AMP_DEV = 32
RES_DEV = 1
INT_DEV = 1
AMP_ALL = 4096
RES_ALL = 128
INT_BLOCKS = 8
N_GRP = 8
N_WIDE = 16
DEVICES = 128


def spread_holders(counts, usable, slot_index, subkey):
    ends = jnp.cumsum(counts, axis=2)
    sorted_holder = jnp.sum((slot_index[None, None, :, None] >= ends[:, :, None, :]).astype(jnp.int32), axis=3)
    sorted_holder = jnp.minimum(sorted_holder, N_WIDE - 1).astype(jnp.int32)
    scores = jax.random.randint(subkey, usable.shape, 0, 1 << 20) * TASK_SLOTS + slot_index[None, None, :]
    scores = jnp.where(usable, scores, (1 << 20) * TASK_SLOTS + slot_index[None, None, :])
    order_of = jnp.argsort(scores, axis=2)
    return jnp.take_along_axis(sorted_holder, order_of, axis=2)


def layout(key):
    keys = jax.random.split(jax.random.fold_in(key, 101), 9)
    bucket = TASK_SLOTS // N_WIDE
    lane_ids = jnp.arange(N_WIDE, dtype=jnp.int32)
    busy_lane = jax.random.randint(keys[0], (N_GRP,), 0, N_WIDE)
    light_lane = (busy_lane + 1 + jax.random.randint(keys[8], (N_GRP,), 0, N_WIDE - 1)) % N_WIDE
    counts = jax.random.randint(keys[1], (N_GRP, N_WIDE, N_WIDE), 0, bucket + 1)
    full_mask = (lane_ids[None, None, :] == busy_lane[:, None, None]) | (lane_ids[None, :, None] == busy_lane[:, None, None])
    counts = jnp.where(full_mask, bucket, counts).astype(jnp.int32)
    light_mask = (lane_ids[None, :, None] == light_lane[:, None, None]) & (lane_ids[None, None, :] != busy_lane[:, None, None])
    counts = jnp.where(light_mask, 0, counts).astype(jnp.int32)
    owner_shuffle = jax.vmap(lambda subkey: jax.random.permutation(subkey, N_WIDE))(jax.random.split(keys[2], N_GRP))
    inverse = jnp.argsort(owner_shuffle, axis=1)
    res_counts = jnp.take_along_axis(counts, jnp.broadcast_to(inverse[:, None, :], counts.shape), axis=2)
    totals = jnp.sum(counts, axis=2).astype(jnp.int32)
    slot_index = jnp.arange(TASK_SLOTS, dtype=jnp.int32)
    usable = slot_index[None, None, :] < totals[:, :, None]
    amp_holder = spread_holders(counts, usable, slot_index, keys[3])
    res_holder = spread_holders(res_counts, usable, slot_index, keys[4])
    amp_slot = jax.random.randint(keys[5], usable.shape, 0, AMP_DEV)
    res_slot = jax.random.randint(keys[6], usable.shape, 0, RES_DEV)
    task_amp = amp_holder * AMP_DEV + amp_slot
    position = res_holder * RES_DEV + res_slot
    kept = jax.vmap(lambda subkey: jax.random.permutation(subkey, RES_DEV * N_WIDE))(jax.random.split(keys[7], N_GRP))
    kept_wide = jnp.broadcast_to(kept[:, None, :], (N_GRP, N_WIDE, RES_DEV * N_WIDE))
    task_res = jnp.take_along_axis(kept_wide, position, axis=2)
    return (task_amp.reshape(N_GRP * N_WIDE, TASK_SLOTS).astype(jnp.int32), task_res.reshape(N_GRP * N_WIDE, TASK_SLOTS).astype(jnp.int32), totals.reshape(N_GRP * N_WIDE).astype(jnp.int32), kept.astype(jnp.int32))


def draw_task_amp(key, part):
    return layout(key)[0]


def draw_task_res(key, part):
    return layout(key)[1]


def draw_task_count(key, part):
    return layout(key)[2]


def draw_res_owner(key, part):
    return layout(key)[3]


def touch_ends(values, key, least, largest):
    place = [jax.random.randint(jax.random.fold_in(key, axis), (), 0, length) for axis, length in enumerate(values.shape)]
    longest = values.shape.index(max(values.shape))
    beside = place[:longest] + [(place[longest] + 1) % values.shape[longest]] + place[longest + 1:]
    return values.at[tuple(place)].set(least).at[tuple(beside)].set(largest)


def block_levels(stream_key, extent, cuts, low, largest):
    def one(axis_at, shards_of):
        draws = jax.random.uniform(jax.random.fold_in(jax.random.fold_in(stream_key, 6), axis_at), (shards_of,), jnp.float32, low / len(cuts), largest / len(cuts))
        return jnp.repeat(jnp.exp(draws), extent[axis_at] // shards_of).reshape((-1,) + (1,) * (len(extent) - axis_at - 1))

    gain = one(*cuts[0])
    for cut in cuts[1:]:
        gain = gain * one(*cut)
    return gain


def noise(own_key, extent, deviation, most, shards=(), held_as=jnp.bfloat16):
    loudness = block_levels(own_key, extent, shards, -0.22, 0.18) if shards else 1.0
    values = jax.random.normal(own_key, extent, jnp.float32) * deviation * loudness
    return jnp.minimum(jnp.maximum(values, -most), most).astype(held_as)


def setup_inputs(seed: int = 0) -> dict:
    key_list = jax.random.split(jax.random.key(seed), 13)
    amplitudes = noise(key_list[0], (AMP_ALL, TILE_ROWS, BLOCK_COLS), 1.0, 6.0, ((0, 128),), jnp.float32)
    integrals = noise(key_list[1], (INT_BLOCKS, BLOCK_COLS, WINDOW), BLOCK_COLS ** -0.5, 0.25, ((0, 8),), jnp.float32)
    base_residual = noise(key_list[2], (RES_ALL, TILE_ROWS, WINDOW), 1.0, 6.0, ((0, 128),), jnp.float32)
    occ_gap = jnp.clip(0.5 + 3.5 * jax.random.uniform(key_list[3], (RES_ALL, TILE_ROWS), jnp.float32) ** block_levels(key_list[3], (RES_ALL, TILE_ROWS), ((0, 128),), -0.2, 0.2), 0.5, 4.0)
    virt_sum = jnp.clip(jax.random.uniform(key_list[4], (WINDOW,), jnp.float32, 0.5, 4.0), 0.5, 4.0)
    task_amp = draw_task_amp(jax.random.fold_in(key_list[12], 71), 0)
    task_int = touch_ends(jax.random.randint(key_list[6], (DEVICES, TASK_SLOTS), 0, INT_BLOCKS), jax.random.fold_in(key_list[6], 1), 0, INT_BLOCKS - 1).astype(jnp.int32)
    task_res = draw_task_res(jax.random.fold_in(key_list[12], 71), 0)
    task_count = draw_task_count(jax.random.fold_in(key_list[12], 71), 0)
    res_owner = draw_res_owner(jax.random.fold_in(key_list[12], 71), 0)
    amp_label = touch_ends(jax.random.randint(key_list[10], (AMP_ALL,), 0, 4), jax.random.fold_in(key_list[10], 1), 0, 3).astype(jnp.int32)
    int_label = touch_ends(jax.random.randint(key_list[11], (INT_BLOCKS,), 0, 4), jax.random.fold_in(key_list[11], 1), 0, 3).astype(jnp.int32)
    return dict(amplitudes=amplitudes, integrals=integrals, base_residual=base_residual, occ_gap=occ_gap, virt_sum=virt_sum, task_amp=task_amp, task_int=task_int, task_res=task_res, task_count=task_count, res_owner=res_owner, amp_label=amp_label, int_label=int_label)


def reference(amplitudes, integrals, base_residual, occ_gap, virt_sum, task_amp, task_int, task_res, task_count, res_owner, amp_label, int_label):
    row_tiles = AMP_DEV * N_WIDE
    row_res = RES_DEV * N_WIDE
    blocks = INT_DEV * N_GRP
    slot_index = jnp.arange(TASK_SLOTS, dtype=jnp.int32)
    pieces = []
    for row_group in range(N_GRP):
        lanes_of = slice(row_group * N_WIDE, (row_group + 1) * N_WIDE)
        usable = (slot_index[None, :] < task_count[lanes_of][:, None]).reshape(-1)
        amp_ids = (task_amp[lanes_of].reshape(-1) + row_group * row_tiles).astype(jnp.int32)
        int_ids = task_int[lanes_of].reshape(-1).astype(jnp.int32)
        parity = (amp_label[amp_ids] + int_label[int_ids]) % 2
        signs = jnp.where(usable, 1.0 - 2.0 * parity.astype(jnp.float32), 0.0).astype(jnp.float32)
        where_kept = jnp.argsort(res_owner[row_group]).astype(jnp.int32)
        position = where_kept[task_res[lanes_of].reshape(-1)].astype(jnp.int32)
        segment = (position * blocks + int_ids).astype(jnp.int32)
        phased = amplitudes[amp_ids] * signs[:, None, None]
        stacked = jax.ops.segment_sum(phased, segment, num_segments=row_res * blocks)
        stacked = stacked.reshape(row_res, blocks, TILE_ROWS, BLOCK_COLS)
        summed_all = jnp.einsum("pcik,ckl->pil", stacked, integrals, precision=lax.Precision.HIGHEST)
        rows_of = slice(row_group * row_res, (row_group + 1) * row_res)
        divisor = occ_gap[rows_of][:, :, None] + virt_sum[None, None, :]
        pieces.append((base_residual[rows_of] + summed_all) / divisor)
    return jnp.concatenate(pieces, axis=0)
```

```python
import jax
import jax.numpy as jnp
from jax import lax
from jax.experimental import pallas as pl
from jax.experimental.pallas import tpu as pltpu
from jax.sharding import PartitionSpec as P

MESH = pl.DeviceIdType.MESH
f32, bf16, i32 = jnp.float32, jnp.bfloat16, jnp.int32


def iota(shape, dim):
    return lax.broadcasted_iota(i32, shape, dim)


def split(v):
    hi = v.astype(bf16)
    return hi, (v - hi.astype(f32)).astype(bf16)


def mm(a, b):
    return jnp.dot(a, b, preferred_element_type=f32)


def kernel(
    amp,
    integ,
    base,
    pack,
    out,
    a_buf,
    ib,
    shi,
    slo,
    tk,
    acc,
    tb,
    rbuf,
    a_sem,
    own_sem,
    t_send,
    t_recv,
    x_send,
    x_recv,
    q_send,
    q_recv,
    c_send,
    c_recv,
    r_send,
    r_recv,
):
    g = lax.axis_index("grp")
    w = lax.axis_index("wide")
    x, s = g // 2, g % 2
    z, y = w // 4, w % 4
    par = (y + z) % 2
    right = {"grp": ((x + 1) % 4) * 2 + s, "wide": w}
    left = {"grp": ((x + 3) % 4) * 2 + s, "wide": w}
    twin = {"grp": x * 2 + 1 - s, "wide": w}
    sides = (
        {"grp": g, "wide": z * 4 + (y + 1) % 4},
        {"grp": g, "wide": z * 4 + (y + 3) % 4},
        {"grp": g, "wide": ((z + 1) % 4) * 4 + y},
        {"grp": g, "wide": ((z + 3) % 4) * 4 + y},
    )
    mine = par * 256
    theirs = (1 - par) * 256
    own = g

    def remote(src, dst, send, recv, dev):
        return pltpu.make_async_remote_copy(
            src_ref=src,
            dst_ref=dst,
            send_sem=send,
            recv_sem=recv,
            device_id=dev,
            device_id_type=MESH,
        )

    load = pltpu.make_async_copy(amp, a_buf, a_sem)
    load.start()
    loads = []
    for h in range(2):
        loads.append(
            pltpu.make_async_copy(
                integ.at[0, :, pl.ds(h * 256, 256)], ib.at[h, own], own_sem.at[h]
            )
        )
        loads[h].start()

    barrier = pltpu.get_barrier_semaphore()
    for dev in (right, left, twin):
        pl.semaphore_signal(barrier, inc=1, device_id=dev, device_id_type=MESH)

    def greet(d, _):
        pl.semaphore_signal(
            barrier, inc=1, device_id={"grp": g, "wide": (w + d) % 16}, device_id_type=MESH
        )
        return 0

    lax.fori_loop(1, 16, greet, 0)
    pl.semaphore_wait(barrier, 18)

    def task_copy(d):
        return remote(
            pack, tb.at[w], t_send.at[d], t_recv.at[d], {"grp": g, "wide": (w + d) % 16}
        )

    lax.fori_loop(1, 16, lambda d, _: (task_copy(d).start(), 0)[1], 0)

    hop = ((3, 0), (1, 1), (3, 1), (1, 0), (2, 0), (2, 1))

    def block(k, flip=0):
        return 2 * ((x + hop[k][0]) % 4) + (1 - s if flip else s)

    def rows(k, lo=0, n=128):
        return pl.ds(mine + hop[k][1] * 128 + lo, n)

    def x_own(h, k):
        r = rows(k)
        return remote(
            integ.at[0, r, pl.ds(h * 256, 256)],
            ib.at[h, own, r],
            x_send.at[h, k],
            x_recv.at[h, k],
            right if k in (0, 2) else left,
        )

    def x_relay(h, k):
        part = ib.at[h, block(k), rows(k)]
        return remote(
            part, part, x_send.at[h, k + 4], x_recv.at[h, k + 4], right if k == 0 else left
        )

    def x_in(h, k):
        part = ib.at[h, block(k), rows(k)]
        return remote(part, part, x_send.at[h, k], x_recv.at[h, k], right)

    def side_out(h, k, e):
        part = ib.at[h, block(k), rows(k, e * 64, 64)]
        return remote(
            part, part, q_send.at[h, k, e], q_recv.at[h, k, e], sides[hop[k][1] * 2 + e]
        )

    def side_in(h, k, e):
        part = ib.at[h, block(k), pl.ds(theirs + hop[k][1] * 128 + e * 64, 64)]
        return remote(part, part, q_send.at[h, k, e], q_recv.at[h, k, e], right)

    def twin_x(h, k, flip=0):
        part = ib.at[h, block(k, flip), rows(k)]
        return remote(part, part, c_send.at[h, 1 + k], c_recv.at[h, 1 + k], twin)

    first = (0, 1, 4)
    second = (2, 3, 5)

    def twin_q(h, j, flip=0):
        part = ib.at[h, block(first[j], flip), pl.ds(theirs, 256)]
        return remote(part, part, c_send.at[h, 7 + j], c_recv.at[h, 7 + j], twin)

    def twin_own(h):
        return remote(
            integ.at[0, :, pl.ds(h * 256, 256)],
            ib.at[h, own],
            c_send.at[h, 0],
            c_recv.at[h, 0],
            twin,
        )

    def twin_own_in(h):
        part = ib.at[h, 2 * x + 1 - s]
        return remote(part, part, c_send.at[h, 0], c_recv.at[h, 0], twin)

    def got_x(h, k):
        x_in(h, k).wait_recv()
        if k < 2:
            x_relay(h, k).start()
        side_out(h, k, 0).start()
        side_out(h, k, 1).start()
        twin_x(h, k).start()

    def got_q(h, j):
        for k in (first[j], second[j]):
            for e in range(2):
                side_in(h, k, e).wait_recv()
        twin_q(h, j).start()

    def got_twin(h, j):
        twin_x(h, first[j], 1).wait_recv()
        twin_x(h, second[j], 1).wait_recv()
        twin_q(h, j, 1).wait_recv()

    for k in (0, 1, 2, 3):
        x_own(0, k).start()
    twin_own(0).start()

    lane, row = iota((128, 128), 1), iota((128, 128), 0)

    def column(values, which):
        return jnp.sum(jnp.where(lane == which, values, 0.0), axis=1, keepdims=True)

    owner = column(pack[3:4, :].astype(f32), row % 16).astype(i32)
    sign_c = column((1 - 2 * (pack[5:6, :] & 1)).astype(f32), row // 16)
    sign_b = (1 - 2 * (pack[4:5, :] & 1)).astype(f32)[:, :32]
    which_c = row // 16
    local = iota((32, 128), 0) + w * 32

    def task_in(d):
        return remote(
            pack,
            tb.at[(w - d + 16) % 16],
            t_send.at[d],
            t_recv.at[d],
            {"grp": g, "wide": (w + d) % 16},
        )

    lax.fori_loop(1, 16, lambda d, _: (task_in(d).wait_recv(), 0)[1], 0)
    tb[w] = pack[...]
    hits, picks = [], []
    for v in range(16):
        names = tb[v]
        hits.append(
            jnp.where(
                (names[1:2, :] == which_c) & (names[2:3, :] == owner), 1.0, 0.0
            ).astype(bf16)
        )
        picks.append(jnp.where(names[0:1, :] == local, 1.0, 0.0).astype(bf16))
    t = lax.dot_general(
        jnp.concatenate(hits, axis=1),
        jnp.concatenate(picks, axis=1),
        (((1,), (1,)), ((), ())),
        preferred_element_type=f32,
    )
    t = (t * sign_b * sign_c).astype(bf16)
    spread = jnp.where(iota((32, 256), 0) == iota((32, 256), 1) // 8, 1.0, 0.0).astype(bf16)
    lift = jnp.where(iota((1024, 128), 1) == iota((1024, 128), 0) // 8, 1.0, 0.0).astype(bf16)
    wide_t = mm(lift, mm(t, spread).astype(bf16))
    tk[...] = jnp.where(
        iota((1024, 256), 0) % 8 == iota((1024, 256), 1) % 8, wide_t, 0.0
    ).astype(bf16)

    load.wait()

    def form(i, _):
        @pl.when(i == 1)
        def _():
            got_x(0, 0)
            got_x(0, 1)
            for k in (0, 1, 2, 3):
                x_own(1, k).start()
            twin_own(1).start()

        @pl.when(i == 4)
        def _():
            got_x(0, 2)
            got_x(0, 3)

        part = a_buf[:, pl.ds(pl.multiple_of(i * 8, 8), 8), :].reshape(256, 512)
        hi, lo = split(part)
        both = mm(tk[...], hi) + mm(tk[...], lo)
        hi, lo = split(both)
        shi[:, i] = hi.reshape(8, 128, 512)
        slo[:, i] = lo.reshape(8, 128, 512)
        return 0

    lax.fori_loop(0, 8, form, 0)

    def rs_copy(h, d):
        p = (w + d) % 16
        return remote(
            acc.at[h, :, p],
            rbuf.at[h, d],
            r_send.at[h, d],
            r_recv.at[h, d],
            {"grp": g, "wide": p},
        )

    def rs_start(h):
        lax.fori_loop(1, 16, lambda d, _: (rs_copy(h, d).start(), 0)[1], 0)

    def before(u, fn):
        pl.when(u == fn[0])(fn[1])

    def events(u):
        @pl.when(u == 0)
        def _():
            got_q(0, 0)
            got_q(0, 1)
            loads[0].wait()
            got_x(0, 4)
            got_x(0, 5)

        @pl.when(u == 1)
        def _():
            twin_own_in(0).wait_recv()

        @pl.when(u == 3)
        def _():
            got_twin(0, 0)

        @pl.when(u == 4)
        def _():
            got_q(0, 2)
            got_x(1, 0)
            got_x(1, 1)

        @pl.when(u == 5)
        def _():
            got_twin(0, 1)

        @pl.when(u == 7)
        def _():
            got_twin(0, 2)
            got_x(1, 2)
            got_x(1, 3)

        @pl.when(u == 8)
        def _():
            rs_start(0)
            loads[1].wait()

        @pl.when(u == 9)
        def _():
            twin_own_in(1).wait_recv()

        @pl.when(u == 10)
        def _():
            got_q(1, 0)
            got_q(1, 1)
            got_x(1, 4)
            got_x(1, 5)

        @pl.when(u == 11)
        def _():
            got_twin(1, 0)

        @pl.when(u == 13)
        def _():
            got_twin(1, 1)

        @pl.when(u == 14)
        def _():
            got_q(1, 2)

        @pl.when(u == 15)
        def _():
            got_twin(1, 2)

    acc[...] = jnp.zeros_like(acc)

    def unit(u, _):
        events(u)
        h, v = u // 8, u % 8
        d = v // 2
        far = (4 - (d + d // 2 - 2 * (d // 3))) % 4
        c = 2 * ((x + far) % 4) + (s + v) % 2
        ihi, ilo = split(ib[h, c])
        sh = shi[c].reshape(1024, 512)
        sl = slo[c].reshape(1024, 512)
        prod = mm(sh, ihi) + mm(sh, ilo) + mm(sl, ihi)
        acc[h] = acc[h] + prod.reshape(8, 16, 8, 256)
        return 0

    lax.fori_loop(0, 16, unit, 0)
    rs_start(1)

    for h in range(2):
        lax.fori_loop(1, 16, lambda d, _: (rs_copy(h, d).wait_recv(), 0)[1], 0)
        cols = pl.ds(h * 256, 256)
        out[:, :, cols] = base[:, :, cols] + acc[h, :, w]

        def add(d, _):
            out[:, :, cols] = out[:, :, cols] + rbuf[h, d]
            return 0

        lax.fori_loop(1, 16, add, 0)

    lax.fori_loop(1, 16, lambda d, _: (task_copy(d).wait_send(), 0)[1], 0)
    for h in range(2):
        for k in range(4):
            x_own(h, k).wait_send()
        for k in range(2):
            x_relay(h, k).wait_send()
        for k in range(6):
            side_out(h, k, 0).wait_send()
            side_out(h, k, 1).wait_send()
            twin_x(h, k).wait_send()
        for j in range(3):
            twin_q(h, j).wait_send()
        twin_own(h).wait_send()
        lax.fori_loop(1, 16, lambda d, _: (rs_copy(h, d).wait_send(), 0)[1], 0)


def fused(amplitudes, integrals, base, pack):
    vmem = pl.BlockSpec(memory_space=pltpu.VMEM)
    hbm = pl.BlockSpec(memory_space=pl.ANY)
    dma = pltpu.SemaphoreType.DMA
    return pl.pallas_call(
        kernel,
        out_shape=jax.ShapeDtypeStruct((8, 8, 512), f32),
        in_specs=[hbm, hbm, vmem, vmem],
        out_specs=vmem,
        scratch_shapes=[
            pltpu.VMEM((32, 64, 512), f32),
            pltpu.VMEM((2, 8, 512, 256), f32),
            pltpu.VMEM((8, 8, 128, 512), bf16),
            pltpu.VMEM((8, 8, 128, 512), bf16),
            pltpu.VMEM((1024, 256), bf16),
            pltpu.VMEM((2, 8, 16, 8, 256), f32),
            pltpu.VMEM((16, 8, 128), i32),
            pltpu.VMEM((2, 16, 8, 8, 256), f32),
            dma,
            dma((2,)),
            dma((16,)),
            dma((16,)),
            dma((2, 6)),
            dma((2, 6)),
            dma((2, 6, 2)),
            dma((2, 6, 2)),
            dma((2, 10)),
            dma((2, 10)),
            dma((2, 16)),
            dma((2, 16)),
        ],
        compiler_params=pltpu.CompilerParams(
            collective_id=0, has_side_effects=True, vmem_limit_bytes=60 * 2**20
        ),
    )(amplitudes, integrals, base, pack)


def line(values):
    return jnp.pad(values, (0, 128 - values.shape[0]))[None]


def on_device(
    amplitudes,
    integrals,
    base_residual,
    occ_gap,
    virt_sum,
    task_amp,
    task_int,
    task_res,
    task_count,
    res_owner,
    amp_label,
    int_label,
):
    slot = jnp.arange(128, dtype=i32)[None]
    amp = jnp.where(slot < task_count[0], line(task_amp[0]), -1)
    pack = jnp.concatenate(
        [
            amp,
            line(task_int[0]),
            line(task_res[0]),
            line(res_owner[0]),
            line(amp_label),
            line(int_label),
            jnp.zeros((2, 128), i32),
        ],
        axis=0,
    )
    summed = fused(amplitudes, integrals, base_residual.reshape(8, 8, 512), pack)
    divisor = occ_gap[:, :, None] + virt_sum[None, None, :]
    return summed.reshape(1, 64, 512) / divisor


def solution(mesh):
    both = ("grp", "wide")
    return jax.shard_map(
        on_device,
        mesh=mesh,
        in_specs=(
            P(both, None, None),
            P("grp", None, None),
            P(both, None, None),
            P(both, None),
            P(),
            P(both, None),
            P(both, None),
            P(both, None),
            P(both),
            P("grp", None),
            P(both),
            P(),
        ),
        out_specs=P(both, None, None),
        check_vma=False,
    )
```

```python
import jax
import jax.numpy as jnp
from jax import lax
from jax.experimental import pallas as pl
from jax.experimental.pallas import tpu as pltpu
from jax.sharding import PartitionSpec as P

MESH = pl.DeviceIdType.MESH
f32, bf16, i32 = jnp.float32, jnp.bfloat16, jnp.int32


def iota(shape, dim):
    return lax.broadcasted_iota(i32, shape, dim)


def split(v):
    hi = v.astype(bf16)
    return hi, (v - hi.astype(f32)).astype(bf16)


def mm(a, b):
    return jnp.dot(a, b, preferred_element_type=f32)


def kernel(
    amp,
    integ,
    base,
    pack,
    out,
    a_buf,
    ib,
    shi,
    slo,
    tk,
    acc,
    tb,
    far,
    near,
    fin,
    a_sem,
    own_sem,
    t_send,
    t_recv,
    x_send,
    x_recv,
    q_send,
    q_recv,
    c_send,
    c_recv,
    f_send,
    f_recv,
    n_send,
    n_recv,
    e_send,
    e_recv,
):
    g = lax.axis_index("grp")
    w = lax.axis_index("wide")
    x, s = g // 2, g % 2
    z, y = w // 4, w % 4
    par = (y + z) % 2
    right = {"grp": ((x + 1) % 4) * 2 + s, "wide": w}
    left = {"grp": ((x + 3) % 4) * 2 + s, "wide": w}
    twin = {"grp": x * 2 + 1 - s, "wide": w}
    sides = (
        {"grp": g, "wide": z * 4 + (y + 1) % 4},
        {"grp": g, "wide": z * 4 + (y + 3) % 4},
        {"grp": g, "wide": ((z + 1) % 4) * 4 + y},
        {"grp": g, "wide": ((z + 3) % 4) * 4 + y},
    )
    mine = par * 256
    theirs = (1 - par) * 256
    own = g
    along_z = [{"grp": g, "wide": ((z + d) % 4) * 4 + y} for d in range(4)]
    along_y = [{"grp": g, "wide": z * 4 + (y + d) % 4} for d in range(4)]

    def remote(src, dst, send, recv, dev):
        return pltpu.make_async_remote_copy(
            src_ref=src,
            dst_ref=dst,
            send_sem=send,
            recv_sem=recv,
            device_id=dev,
            device_id_type=MESH,
        )

    load = pltpu.make_async_copy(amp, a_buf, a_sem)
    load.start()
    loads = []
    for h in range(2):
        loads.append(
            pltpu.make_async_copy(
                integ.at[0, :, pl.ds(h * 256, 256)], ib.at[h, own], own_sem.at[h]
            )
        )
        loads[h].start()

    barrier = pltpu.get_barrier_semaphore()
    for dev in (right, left, twin, *along_z[1:], *along_y[1:]):
        pl.semaphore_signal(barrier, inc=1, device_id=dev, device_id_type=MESH)
    pl.semaphore_wait(barrier, 9)

    def task_z(d, back=0):
        return remote(
            pack, tb.at[y, (z - d if back else z) % 4], t_send.at[d], t_recv.at[d], along_z[d]
        )

    def task_y(d, back=0):
        part = tb.at[(y - d if back else y) % 4]
        return remote(part, part, t_send.at[4 + d], t_recv.at[4 + d], along_y[d])

    for d in (2, 1, 3):
        task_z(d).start()
    keep = pltpu.make_async_copy(pack, tb.at[y, z], t_send.at[0])
    keep.start()

    hop = ((3, 0), (1, 1), (3, 1), (1, 0), (2, 0), (2, 1))

    def block(k, flip=0):
        return 2 * ((x + hop[k][0]) % 4) + (1 - s if flip else s)

    def rows(k, lo=0, n=128):
        return pl.ds(mine + hop[k][1] * 128 + lo, n)

    def x_own(h, k):
        r = rows(k)
        return remote(
            integ.at[0, r, pl.ds(h * 256, 256)],
            ib.at[h, own, r],
            x_send.at[h, k],
            x_recv.at[h, k],
            right if k in (0, 2) else left,
        )

    def x_relay(h, k):
        part = ib.at[h, block(k), rows(k)]
        return remote(
            part, part, x_send.at[h, k + 4], x_recv.at[h, k + 4], right if k == 0 else left
        )

    def x_in(h, k):
        part = ib.at[h, block(k), rows(k)]
        return remote(part, part, x_send.at[h, k], x_recv.at[h, k], right)

    def side_out(h, k, e):
        part = ib.at[h, block(k), rows(k, e * 64, 64)]
        return remote(
            part, part, q_send.at[h, k, e], q_recv.at[h, k, e], sides[hop[k][1] * 2 + e]
        )

    def side_in(h, k, e):
        part = ib.at[h, block(k), pl.ds(theirs + hop[k][1] * 128 + e * 64, 64)]
        return remote(part, part, q_send.at[h, k, e], q_recv.at[h, k, e], right)

    def twin_x(h, k, flip=0):
        part = ib.at[h, block(k, flip), rows(k)]
        return remote(part, part, c_send.at[h, 1 + k], c_recv.at[h, 1 + k], twin)

    first = (0, 1, 4)
    second = (2, 3, 5)

    def twin_q(h, j, flip=0):
        part = ib.at[h, block(first[j], flip), pl.ds(theirs, 256)]
        return remote(part, part, c_send.at[h, 7 + j], c_recv.at[h, 7 + j], twin)

    def twin_own(h):
        return remote(
            integ.at[0, :, pl.ds(h * 256, 256)],
            ib.at[h, own],
            c_send.at[h, 0],
            c_recv.at[h, 0],
            twin,
        )

    def twin_own_in(h):
        part = ib.at[h, 2 * x + 1 - s]
        return remote(part, part, c_send.at[h, 0], c_recv.at[h, 0], twin)

    def got_x(h, k):
        x_in(h, k).wait_recv()
        if k < 2:
            x_relay(h, k).start()
        side_out(h, k, 0).start()
        side_out(h, k, 1).start()
        twin_x(h, k).start()

    def got_q(h, j):
        for k in (first[j], second[j]):
            for e in range(2):
                side_in(h, k, e).wait_recv()
        twin_q(h, j).start()

    def got_twin(h, j):
        twin_x(h, first[j], 1).wait_recv()
        twin_x(h, second[j], 1).wait_recv()
        twin_q(h, j, 1).wait_recv()

    for k in (0, 1, 2, 3):
        x_own(0, k).start()
    twin_own(0).start()

    lane, row = iota((128, 128), 1), iota((128, 128), 0)

    def column(values, which):
        return jnp.sum(jnp.where(lane == which, values, 0.0), axis=1, keepdims=True)

    owner = column(pack[3:4, :].astype(f32), row % 16).astype(i32)
    sign_c = column((1 - 2 * (pack[5:6, :] & 1)).astype(f32), row // 16)
    sign_b = (1 - 2 * (pack[4:5, :] & 1)).astype(f32)[:, :32]
    which_c = row // 16
    local = iota((32, 128), 0) + w * 32
    real = iota((32, 128), 1) < 96

    keep.wait()
    for d in (1, 3, 2):
        task_z(d, 1).wait_recv()
    for d in (2, 1, 3):
        task_y(d).start()
    got_x(0, 0)
    got_x(0, 1)
    for d in (1, 3, 2):
        task_y(d, 1).wait_recv()
    hits, picks = [], []
    for v in range(16):
        names = tb[v // 4, v % 4]
        hits.append(
            jnp.where(
                (names[1:2, :] == which_c) & (names[2:3, :] == owner), 1.0, 0.0
            ).astype(bf16)
        )
        picks.append(
            jnp.where((names[0:1, :] == local) & real, 1.0, 0.0).astype(bf16)
        )
    t = lax.dot_general(
        jnp.concatenate(hits, axis=1),
        jnp.concatenate(picks, axis=1),
        (((1,), (1,)), ((), ())),
        preferred_element_type=f32,
    )
    t = (t * sign_b * sign_c).astype(bf16)
    spread = jnp.where(iota((32, 256), 0) == iota((32, 256), 1) // 8, 1.0, 0.0).astype(bf16)
    lift = jnp.where(iota((1024, 128), 1) == iota((1024, 128), 0) // 8, 1.0, 0.0).astype(bf16)
    wide_t = mm(lift, mm(t, spread).astype(bf16))
    tk[...] = jnp.where(
        iota((1024, 256), 0) % 8 == iota((1024, 256), 1) % 8, wide_t, 0.0
    ).astype(bf16)

    load.wait()

    def form(i, _):
        @pl.when(i == 0)
        def _():
            for k in (0, 1, 2, 3):
                x_own(1, k).start()
            twin_own(1).start()

        @pl.when(i == 3)
        def _():
            got_x(0, 2)
            got_x(0, 3)

        part = a_buf[:, pl.ds(pl.multiple_of(i * 8, 8), 8), :].reshape(256, 512)
        hi, lo = split(part)
        both = mm(tk[...], hi) + mm(tk[...], lo)
        hi, lo = split(both)
        shi[:, i] = hi.reshape(8, 128, 512)
        slo[:, i] = lo.reshape(8, 128, 512)
        return 0

    lax.fori_loop(0, 8, form, 0)

    lo, hi = pl.ds(0, 2), pl.ds(2, 2)
    every = pl.ds(0, 4)

    def part(h, a, f, e):
        if a == 0:
            return (h, slice(None), (z + f) % 4, e, slice(None), pl.ds(0, 128))
        return (h, slice(None), e, (y + f) % 4, slice(None), pl.ds(128, 128))

    def first_axis(a):
        return along_y if a else along_z

    def second_axis(a):
        return along_z if a else along_y

    def rs_far(h, a, v):
        return remote(
            acc.at[part(h, a, 2, hi if v else lo)],
            far.at[h, a, v],
            f_send.at[h, a, v],
            f_recv.at[h, a, v],
            first_axis(a)[3 if v else 1],
        )

    def rs_near(h, a, v, late):
        e = (lo, hi)[1 - v] if not late else (lo, hi)[v]
        return remote(
            acc.at[part(h, a, 3 if v else 1, e)],
            near.at[h, a, v, :, e],
            n_send.at[h, a, v, late],
            n_recv.at[h, a, v, late],
            first_axis(a)[3 if v else 1],
        )

    def rs_last(h, a, d):
        to = (slice(None), ((z if a else y) + d) % 4)
        return remote(
            near.at[(h, a, 0) + to],
            fin.at[h, a, d],
            e_send.at[h, a, d],
            e_recv.at[h, a, d],
            second_axis(a)[d],
        )

    ways = [(a, v) for v in range(2) for a in range(2)]

    def rs_one(h):
        for a, v in ways:
            rs_far(h, a, v).start()
        for a, v in ways:
            rs_near(h, a, v, 0).start()

    def rs_two(h):
        for a, v in ways:
            rs_far(h, a, v).wait_recv()
            at = part(h, a, 3 if v else 1, hi if v else lo)
            acc[at] = acc[at] + far[h, a, v]
        for a, v in ways:
            rs_near(h, a, v, 1).start()

    def rs_three(h):
        for a in range(2):
            for v in range(2):
                for late in range(2):
                    rs_near(h, a, v, late).wait_recv()
            near[h, a, 0] = near[h, a, 0] + near[h, a, 1] + acc[part(h, a, 0, every)]
        for d in (2, 1, 3):
            for a in range(2):
                rs_last(h, a, d).start()

    def rs_end(h):
        for a in range(2):
            for d in (1, 3, 2):
                rs_last(h, a, d).wait_recv()
            cols = pl.ds(h * 256 + a * 128, 128)
            out[:, :, cols] = (
                base[:, :, cols]
                + near[h, a, 0, :, z if a else y]
                + fin[h, a, 1]
                + fin[h, a, 2]
                + fin[h, a, 3]
            )

    def events(u):
        if u == 0:
            got_x(0, 4)
            got_x(0, 5)
            got_q(0, 0)
            got_q(0, 1)
            loads[0].wait()
        if u == 1:
            twin_own_in(0).wait_recv()
        if u == 3:
            got_twin(0, 0)
            got_x(1, 0)
            got_x(1, 1)
        if u == 4:
            got_q(0, 2)
        if u == 5:
            got_twin(0, 1)
        if u == 7:
            got_twin(0, 2)
            got_x(1, 2)
            got_x(1, 3)
        if u == 8:
            rs_one(0)
            loads[1].wait()
        if u == 9:
            twin_own_in(1).wait_recv()
        if u == 10:
            got_q(1, 0)
            got_q(1, 1)
        if u == 11:
            got_twin(1, 0)
        if u == 12:
            got_x(1, 4)
            got_x(1, 5)
        if u == 13:
            got_twin(1, 1)
            rs_two(0)
        if u == 14:
            got_q(1, 2)
        if u == 15:
            got_twin(1, 2)

    for u in range(16):
        events(u)
        h, v = u // 8, u % 8
        c = 2 * ((x + (0, 3, 1, 2)[v // 2]) % 4) + (1 - s if v % 2 else s)
        ihi, ilo = split(ib[h, c])
        sh = shi[c].reshape(1024, 512)
        sl = slo[c].reshape(1024, 512)
        prod = (mm(sh, ihi) + mm(sh, ilo) + mm(sl, ihi)).reshape(8, 4, 4, 8, 256)
        acc[h] = prod if v == 0 else acc[h] + prod

    rs_one(1)
    rs_three(0)
    rs_two(1)
    rs_end(0)
    rs_three(1)
    rs_end(1)

    for d in (1, 2, 3):
        task_z(d).wait_send()
        task_y(d).wait_send()
    for h in range(2):
        for k in range(4):
            x_own(h, k).wait_send()
        for k in range(2):
            x_relay(h, k).wait_send()
        for k in range(6):
            side_out(h, k, 0).wait_send()
            side_out(h, k, 1).wait_send()
            twin_x(h, k).wait_send()
        for j in range(3):
            twin_q(h, j).wait_send()
        twin_own(h).wait_send()
        for a, v in ways:
            rs_far(h, a, v).wait_send()
            rs_near(h, a, v, 0).wait_send()
            rs_near(h, a, v, 1).wait_send()
        for a in range(2):
            for d in (1, 2, 3):
                rs_last(h, a, d).wait_send()


def fused(amplitudes, integrals, base, pack):
    vmem = pl.BlockSpec(memory_space=pltpu.VMEM)
    hbm = pl.BlockSpec(memory_space=pl.ANY)
    dma = pltpu.SemaphoreType.DMA
    return pl.pallas_call(
        kernel,
        out_shape=jax.ShapeDtypeStruct((8, 8, 512), f32),
        in_specs=[hbm, hbm, vmem, vmem],
        out_specs=vmem,
        scratch_shapes=[
            pltpu.VMEM((32, 64, 512), f32),
            pltpu.VMEM((2, 8, 512, 256), f32),
            pltpu.VMEM((8, 8, 128, 512), bf16),
            pltpu.VMEM((8, 8, 128, 512), bf16),
            pltpu.VMEM((1024, 256), bf16),
            pltpu.VMEM((2, 8, 4, 4, 8, 256), f32),
            pltpu.VMEM((4, 4, 8, 128), i32),
            pltpu.VMEM((2, 2, 2, 8, 2, 8, 128), f32),
            pltpu.VMEM((2, 2, 2, 8, 4, 8, 128), f32),
            pltpu.VMEM((2, 2, 4, 8, 8, 128), f32),
            dma,
            dma((2,)),
            dma((8,)),
            dma((8,)),
            dma((2, 6)),
            dma((2, 6)),
            dma((2, 6, 2)),
            dma((2, 6, 2)),
            dma((2, 10)),
            dma((2, 10)),
            dma((2, 2, 2)),
            dma((2, 2, 2)),
            dma((2, 2, 2, 2)),
            dma((2, 2, 2, 2)),
            dma((2, 2, 4)),
            dma((2, 2, 4)),
        ],
        compiler_params=pltpu.CompilerParams(
            collective_id=0, has_side_effects=True, vmem_limit_bytes=60 * 2**20
        ),
    )(amplitudes, integrals, base, pack)


def line(values, row):
    values = values.reshape(1, -1)
    return jnp.pad(values, ((row, 7 - row), (0, 128 - values.shape[1])))


def on_device(
    amplitudes,
    integrals,
    base_residual,
    occ_gap,
    virt_sum,
    task_amp,
    task_int,
    task_res,
    task_count,
    res_owner,
    amp_label,
    int_label,
):
    used = jnp.arange(96, dtype=i32)[None] < task_count[0]
    pack = (
        line(jnp.where(used, task_amp, -1), 0)
        + line(task_int, 1)
        + line(task_res, 2)
        + line(res_owner, 3)
        + line(amp_label, 4)
        + line(int_label, 5)
    )
    summed = fused(amplitudes, integrals, base_residual.reshape(8, 8, 512), pack)
    divisor = occ_gap[:, :, None] + virt_sum[None, None, :]
    return summed.reshape(1, 64, 512) / divisor


def solution(mesh):
    both = ("grp", "wide")
    return jax.shard_map(
        on_device,
        mesh=mesh,
        in_specs=(
            P(both, None, None),
            P("grp", None, None),
            P(both, None, None),
            P(both, None),
            P(),
            P(both, None),
            P(both, None),
            P(both, None),
            P(both),
            P("grp", None),
            P(both),
            P(),
        ),
        out_specs=P(both, None, None),
        check_vma=False,
    )
```

```python
import jax
import jax.numpy as jnp
from jax import lax
from jax.experimental import pallas as pl
from jax.experimental.pallas import tpu as pltpu
from jax.sharding import PartitionSpec as P

MESH = pl.DeviceIdType.MESH
f32, bf16, i32 = jnp.float32, jnp.bfloat16, jnp.int32


def iota(shape, dim):
    return lax.broadcasted_iota(i32, shape, dim)


def split(v):
    hi = v.astype(bf16)
    return hi, (v - hi.astype(f32)).astype(bf16)


def mm(a, b):
    return jnp.dot(a, b, preferred_element_type=f32)


def kernel(
    amp,
    integ,
    base,
    pack,
    out,
    a_buf,
    ib,
    shi,
    slo,
    tk,
    acc,
    tb,
    far,
    near,
    fin,
    a_sem,
    own_sem,
    t_send,
    t_recv,
    x_send,
    x_recv,
    q_send,
    q_recv,
    c_send,
    c_recv,
    f_send,
    f_recv,
    n_send,
    n_recv,
    e_send,
    e_recv,
):
    g = lax.axis_index("grp")
    w = lax.axis_index("wide")
    x, s = g // 2, g % 2
    z, y = w // 4, w % 4
    par = (y + z) % 2
    right = {"grp": ((x + 1) % 4) * 2 + s, "wide": w}
    left = {"grp": ((x + 3) % 4) * 2 + s, "wide": w}
    twin = {"grp": x * 2 + 1 - s, "wide": w}
    sides = (
        {"grp": g, "wide": z * 4 + (y + 1) % 4},
        {"grp": g, "wide": z * 4 + (y + 3) % 4},
        {"grp": g, "wide": ((z + 1) % 4) * 4 + y},
        {"grp": g, "wide": ((z + 3) % 4) * 4 + y},
    )
    mine = par * 256
    theirs = (1 - par) * 256
    own = g
    along_z = [{"grp": g, "wide": ((z + d) % 4) * 4 + y} for d in range(4)]
    along_y = [{"grp": g, "wide": z * 4 + (y + d) % 4} for d in range(4)]

    def remote(src, dst, send, recv, dev):
        return pltpu.make_async_remote_copy(
            src_ref=src,
            dst_ref=dst,
            send_sem=send,
            recv_sem=recv,
            device_id=dev,
            device_id_type=MESH,
        )

    load = pltpu.make_async_copy(amp, a_buf, a_sem)
    load.start()
    loads = []
    for h in range(2):
        loads.append(
            pltpu.make_async_copy(
                integ.at[0, :, pl.ds(h * 256, 256)], ib.at[h, own], own_sem.at[h]
            )
        )
        loads[h].start()

    barrier = pltpu.get_barrier_semaphore()
    for dev in (right, left, twin, *along_z[1:], *along_y[1:]):
        pl.semaphore_signal(barrier, inc=1, device_id=dev, device_id_type=MESH)
    pl.semaphore_wait(barrier, 9)

    def task_z(d, back=0):
        return remote(
            pack, tb.at[y, (z - d if back else z) % 4], t_send.at[d], t_recv.at[d], along_z[d]
        )

    def task_y(d, back=0):
        part = tb.at[(y - d if back else y) % 4]
        return remote(part, part, t_send.at[4 + d], t_recv.at[4 + d], along_y[d])

    for d in (2, 1, 3):
        task_z(d).start()
    keep = pltpu.make_async_copy(pack, tb.at[y, z], t_send.at[0])
    keep.start()

    hop = ((3, 0), (1, 1), (3, 1), (1, 0), (2, 0), (2, 1))

    def block(k, flip=0):
        return 2 * ((x + hop[k][0]) % 4) + (1 - s if flip else s)

    def rows(k, lo=0, n=128):
        return pl.ds(mine + hop[k][1] * 128 + lo, n)

    def x_own(h, k):
        r = rows(k)
        return remote(
            integ.at[0, r, pl.ds(h * 256, 256)],
            ib.at[h, own, r],
            x_send.at[h, k],
            x_recv.at[h, k],
            right if k in (0, 2) else left,
        )

    def x_relay(h, k):
        part = ib.at[h, block(k), rows(k)]
        return remote(
            part, part, x_send.at[h, k + 4], x_recv.at[h, k + 4], right if k == 0 else left
        )

    def x_in(h, k):
        part = ib.at[h, block(k), rows(k)]
        return remote(part, part, x_send.at[h, k], x_recv.at[h, k], right)

    def side_out(h, k, e):
        part = ib.at[h, block(k), rows(k, e * 64, 64)]
        return remote(
            part, part, q_send.at[h, k, e], q_recv.at[h, k, e], sides[hop[k][1] * 2 + e]
        )

    def side_in(h, k, e):
        part = ib.at[h, block(k), pl.ds(theirs + hop[k][1] * 128 + e * 64, 64)]
        return remote(part, part, q_send.at[h, k, e], q_recv.at[h, k, e], right)

    def twin_x(h, k, flip=0):
        part = ib.at[h, block(k, flip), rows(k)]
        return remote(part, part, c_send.at[h, 1 + k], c_recv.at[h, 1 + k], twin)

    first = (0, 1, 4)
    second = (2, 3, 5)

    def twin_q(h, j, flip=0):
        part = ib.at[h, block(first[j], flip), pl.ds(theirs, 256)]
        return remote(part, part, c_send.at[h, 7 + j], c_recv.at[h, 7 + j], twin)

    def twin_own(h):
        return remote(
            integ.at[0, :, pl.ds(h * 256, 256)],
            ib.at[h, own],
            c_send.at[h, 0],
            c_recv.at[h, 0],
            twin,
        )

    def twin_own_in(h):
        part = ib.at[h, 2 * x + 1 - s]
        return remote(part, part, c_send.at[h, 0], c_recv.at[h, 0], twin)

    def got_x(h, k):
        x_in(h, k).wait_recv()
        if k < 2:
            x_relay(h, k).start()
        side_out(h, k, 0).start()
        side_out(h, k, 1).start()
        twin_x(h, k).start()

    def got_q(h, j):
        for k in (first[j], second[j]):
            for e in range(2):
                side_in(h, k, e).wait_recv()
        twin_q(h, j).start()

    def got_twin(h, j):
        twin_x(h, first[j], 1).wait_recv()
        twin_x(h, second[j], 1).wait_recv()
        twin_q(h, j, 1).wait_recv()

    for k in (0, 1, 2, 3):
        x_own(0, k).start()
    twin_own(0).start()

    lane, row = iota((128, 128), 1), iota((128, 128), 0)

    def column(values, which):
        return jnp.sum(jnp.where(lane == which, values, 0.0), axis=1, keepdims=True)

    owner = column(pack[3:4, :].astype(f32), row % 16).astype(i32)
    sign_c = column((1 - 2 * (pack[5:6, :] & 1)).astype(f32), row // 16)
    sign_b = (1 - 2 * (pack[4:5, :] & 1)).astype(f32)[:, :32]
    which_c = row // 16
    local = iota((32, 128), 0) + w * 32
    real = iota((32, 128), 1) < 96

    keep.wait()
    for d in (1, 3, 2):
        task_z(d, 1).wait_recv()
    for d in (2, 1, 3):
        task_y(d).start()
    got_x(0, 0)
    got_x(0, 1)
    for d in (1, 3, 2):
        task_y(d, 1).wait_recv()
    hits, picks = [], []
    for v in range(16):
        names = tb[v // 4, v % 4]
        hits.append(
            jnp.where(
                (names[1:2, :] == which_c) & (names[2:3, :] == owner), 1.0, 0.0
            ).astype(bf16)
        )
        picks.append(
            jnp.where((names[0:1, :] == local) & real, 1.0, 0.0).astype(bf16)
        )
    t = lax.dot_general(
        jnp.concatenate(hits, axis=1),
        jnp.concatenate(picks, axis=1),
        (((1,), (1,)), ((), ())),
        preferred_element_type=f32,
    )
    t = (t * sign_b * sign_c).astype(bf16)
    spread = jnp.where(iota((32, 256), 0) == iota((32, 256), 1) // 8, 1.0, 0.0).astype(bf16)
    lift = jnp.where(iota((1024, 128), 1) == iota((1024, 128), 0) // 8, 1.0, 0.0).astype(bf16)
    wide_t = mm(lift, mm(t, spread).astype(bf16))
    tk[...] = jnp.where(
        iota((1024, 256), 0) % 8 == iota((1024, 256), 1) % 8, wide_t, 0.0
    ).astype(bf16)

    load.wait()

    def form(i, _):
        @pl.when(i == 0)
        def _():
            for k in (0, 1, 2, 3):
                x_own(1, k).start()
            twin_own(1).start()

        @pl.when(i == 3)
        def _():
            got_x(0, 2)
            got_x(0, 3)

        part = a_buf[:, pl.ds(pl.multiple_of(i * 8, 8), 8), :].reshape(256, 512)
        hi, lo = split(part)
        both = mm(tk[...], hi) + mm(tk[...], lo)
        hi, lo = split(both)
        shi[:, i] = hi.reshape(8, 128, 512)
        slo[:, i] = lo.reshape(8, 128, 512)
        return 0

    lax.fori_loop(0, 8, form, 0)

    lo, hi = pl.ds(0, 2), pl.ds(2, 2)
    every = pl.ds(0, 4)

    def part(h, a, f, e):
        if a == 0:
            return (h, slice(None), (z + f) % 4, e, slice(None), pl.ds(0, 128))
        return (h, slice(None), e, (y + f) % 4, slice(None), pl.ds(128, 128))

    def first_axis(a):
        return along_y if a else along_z

    def second_axis(a):
        return along_z if a else along_y

    def rs_far(h, a, v):
        return remote(
            acc.at[part(h, a, 2, hi if v else lo)],
            far.at[h, a, v],
            f_send.at[h, a, v],
            f_recv.at[h, a, v],
            first_axis(a)[3 if v else 1],
        )

    def rs_near(h, a, v, late):
        e = (lo, hi)[1 - v] if not late else (lo, hi)[v]
        return remote(
            acc.at[part(h, a, 3 if v else 1, e)],
            near.at[h, a, v, :, e],
            n_send.at[h, a, v, late],
            n_recv.at[h, a, v, late],
            first_axis(a)[3 if v else 1],
        )

    def rs_last(h, a, d):
        to = (slice(None), ((z if a else y) + d) % 4)
        return remote(
            near.at[(h, a, 0) + to],
            fin.at[h, a, d],
            e_send.at[h, a, d],
            e_recv.at[h, a, d],
            second_axis(a)[d],
        )

    ways = [(a, v) for v in range(2) for a in range(2)]

    def rs_one(h):
        for a, v in ways:
            rs_far(h, a, v).start()
        for a, v in ways:
            rs_near(h, a, v, 0).start()

    def rs_two(h):
        for a, v in ways:
            rs_far(h, a, v).wait_recv()
            at = part(h, a, 3 if v else 1, hi if v else lo)
            acc[at] = acc[at] + far[h, a, v]
        for a, v in ways:
            rs_near(h, a, v, 1).start()

    def rs_three(h):
        for a in range(2):
            for v in range(2):
                for late in range(2):
                    rs_near(h, a, v, late).wait_recv()
            near[h, a, 0] = near[h, a, 0] + near[h, a, 1] + acc[part(h, a, 0, every)]
        for d in (2, 1, 3):
            for a in range(2):
                rs_last(h, a, d).start()

    def rs_end(h):
        for a in range(2):
            for d in (1, 3, 2):
                rs_last(h, a, d).wait_recv()
            cols = pl.ds(h * 256 + a * 128, 128)
            out[:, :, cols] = (
                base[:, :, cols]
                + near[h, a, 0, :, z if a else y]
                + fin[h, a, 1]
                + fin[h, a, 2]
                + fin[h, a, 3]
            )

    def events(u):
        if u == 0:
            got_x(0, 4)
            got_x(0, 5)
            got_q(0, 0)
            got_q(0, 1)
            loads[0].wait()
        if u == 1:
            twin_own_in(0).wait_recv()
        if u == 3:
            got_twin(0, 0)
            got_x(1, 0)
            got_x(1, 1)
        if u == 4:
            got_q(0, 2)
        if u == 5:
            got_twin(0, 1)
        if u == 7:
            got_twin(0, 2)
            got_x(1, 2)
            got_x(1, 3)
        if u == 8:
            rs_one(0)
            loads[1].wait()
        if u == 9:
            twin_own_in(1).wait_recv()
        if u == 10:
            got_q(1, 0)
            got_q(1, 1)
        if u == 11:
            got_twin(1, 0)
        if u == 12:
            got_x(1, 4)
            got_x(1, 5)
        if u == 13:
            got_twin(1, 1)
            rs_two(0)
        if u == 14:
            got_q(1, 2)
        if u == 15:
            got_twin(1, 2)

    for u in range(16):
        events(u)
        h, v = u // 8, u % 8
        c = 2 * ((x + (0, 3, 1, 2)[v // 2]) % 4) + (1 - s if v % 2 else s)
        ihi, ilo = split(ib[h, c])
        for r in (slice(0, 4), slice(4, 8)):
            sh = shi[c, r].reshape(512, 512)
            sl = slo[c, r].reshape(512, 512)
            prod = (mm(sh, ihi) + mm(sh, ilo) + mm(sl, ihi)).reshape(4, 4, 4, 8, 256)
            acc[h, r] = prod if v == 0 else acc[h, r] + prod

    rs_one(1)
    rs_three(0)
    rs_two(1)
    rs_end(0)
    rs_three(1)
    rs_end(1)

    for d in (1, 2, 3):
        task_z(d).wait_send()
        task_y(d).wait_send()
    for h in range(2):
        for k in range(4):
            x_own(h, k).wait_send()
        for k in range(2):
            x_relay(h, k).wait_send()
        for k in range(6):
            side_out(h, k, 0).wait_send()
            side_out(h, k, 1).wait_send()
            twin_x(h, k).wait_send()
        for j in range(3):
            twin_q(h, j).wait_send()
        twin_own(h).wait_send()
        for a, v in ways:
            rs_far(h, a, v).wait_send()
            rs_near(h, a, v, 0).wait_send()
            rs_near(h, a, v, 1).wait_send()
        for a in range(2):
            for d in (1, 2, 3):
                rs_last(h, a, d).wait_send()


def fused(amplitudes, integrals, base, pack):
    vmem = pl.BlockSpec(memory_space=pltpu.VMEM)
    hbm = pl.BlockSpec(memory_space=pl.ANY)
    dma = pltpu.SemaphoreType.DMA
    return pl.pallas_call(
        kernel,
        out_shape=jax.ShapeDtypeStruct((8, 8, 512), f32),
        in_specs=[hbm, hbm, vmem, vmem],
        out_specs=vmem,
        scratch_shapes=[
            pltpu.VMEM((32, 64, 512), f32),
            pltpu.VMEM((2, 8, 512, 256), f32),
            pltpu.VMEM((8, 8, 128, 512), bf16),
            pltpu.VMEM((8, 8, 128, 512), bf16),
            pltpu.VMEM((1024, 256), bf16),
            pltpu.VMEM((2, 8, 4, 4, 8, 256), f32),
            pltpu.VMEM((4, 4, 8, 128), i32),
            pltpu.VMEM((2, 2, 2, 8, 2, 8, 128), f32),
            pltpu.VMEM((2, 2, 2, 8, 4, 8, 128), f32),
            pltpu.VMEM((2, 2, 4, 8, 8, 128), f32),
            dma,
            dma((2,)),
            dma((8,)),
            dma((8,)),
            dma((2, 6)),
            dma((2, 6)),
            dma((2, 6, 2)),
            dma((2, 6, 2)),
            dma((2, 10)),
            dma((2, 10)),
            dma((2, 2, 2)),
            dma((2, 2, 2)),
            dma((2, 2, 2, 2)),
            dma((2, 2, 2, 2)),
            dma((2, 2, 4)),
            dma((2, 2, 4)),
        ],
        compiler_params=pltpu.CompilerParams(
            collective_id=0, has_side_effects=True, vmem_limit_bytes=60 * 2**20
        ),
    )(amplitudes, integrals, base, pack)


def line(values, row):
    values = values.reshape(1, -1)
    return jnp.pad(values, ((row, 7 - row), (0, 128 - values.shape[1])))


def on_device(
    amplitudes,
    integrals,
    base_residual,
    occ_gap,
    virt_sum,
    task_amp,
    task_int,
    task_res,
    task_count,
    res_owner,
    amp_label,
    int_label,
):
    used = jnp.arange(96, dtype=i32)[None] < task_count[0]
    pack = (
        line(jnp.where(used, task_amp, -1), 0)
        + line(task_int, 1)
        + line(task_res, 2)
        + line(res_owner, 3)
        + line(amp_label, 4)
        + line(int_label, 5)
    )
    summed = fused(amplitudes, integrals, base_residual.reshape(8, 8, 512), pack)
    divisor = occ_gap[:, :, None] + virt_sum[None, None, :]
    return summed.reshape(1, 64, 512) / divisor


def solution(mesh):
    both = ("grp", "wide")
    return jax.shard_map(
        on_device,
        mesh=mesh,
        in_specs=(
            P(both, None, None),
            P("grp", None, None),
            P(both, None, None),
            P(both, None),
            P(),
            P(both, None),
            P(both, None),
            P(both, None),
            P(both),
            P("grp", None),
            P(both),
            P(),
        ),
        out_specs=P(both, None, None),
        check_vma=False,
    )
```

```python
import jax
import jax.numpy as jnp
from jax import lax
from jax.experimental import pallas as pl
from jax.experimental.pallas import tpu as pltpu
from jax.sharding import PartitionSpec as P

MESH = pl.DeviceIdType.MESH
f32, bf16, i32 = jnp.float32, jnp.bfloat16, jnp.int32


def iota(shape, dim):
    return lax.broadcasted_iota(i32, shape, dim)


def split(v):
    hi = v.astype(bf16)
    return hi, (v - hi.astype(f32)).astype(bf16)


def mm(a, b):
    return jnp.dot(a, b, preferred_element_type=f32)


def kernel(
    amp,
    integ,
    base,
    pack,
    out,
    a_buf,
    ib,
    shi,
    slo,
    tk,
    acc,
    tb,
    near,
    fin,
    a_sem,
    own_sem,
    t_send,
    t_recv,
    x_send,
    x_recv,
    q_send,
    q_recv,
    c_send,
    c_recv,
    n_send,
    n_recv,
    e_send,
    e_recv,
    ok_sem,
):
    g = lax.axis_index("grp")
    w = lax.axis_index("wide")
    x, s = g // 2, g % 2
    z, y = w // 4, w % 4
    par = (y + z) % 2
    right = {"grp": ((x + 1) % 4) * 2 + s, "wide": w}
    left = {"grp": ((x + 3) % 4) * 2 + s, "wide": w}
    twin = {"grp": x * 2 + 1 - s, "wide": w}
    sides = (
        {"grp": g, "wide": z * 4 + (y + 1) % 4},
        {"grp": g, "wide": z * 4 + (y + 3) % 4},
        {"grp": g, "wide": ((z + 1) % 4) * 4 + y},
        {"grp": g, "wide": ((z + 3) % 4) * 4 + y},
    )
    mine = par * 256
    theirs = (1 - par) * 256
    own = g
    along_z = [{"grp": g, "wide": ((z + d) % 4) * 4 + y} for d in range(4)]
    along_y = [{"grp": g, "wide": z * 4 + (y + d) % 4} for d in range(4)]

    def remote(src, dst, send, recv, dev):
        return pltpu.make_async_remote_copy(
            src_ref=src,
            dst_ref=dst,
            send_sem=send,
            recv_sem=recv,
            device_id=dev,
            device_id_type=MESH,
        )

    load = pltpu.make_async_copy(amp, a_buf, a_sem)
    load.start()
    loads = []
    for h in range(2):
        loads.append(
            pltpu.make_async_copy(
                integ.at[0, :, pl.ds(h * 256, 256)], ib.at[h, own], own_sem.at[h]
            )
        )
        loads[h].start()

    barrier = pltpu.get_barrier_semaphore()
    for dev in (right, left, twin, *along_z[1:], *along_y[1:]):
        pl.semaphore_signal(barrier, inc=1, device_id=dev, device_id_type=MESH)
    pl.semaphore_wait(barrier, 9)

    for d in range(1, 4):
        pl.semaphore_signal(ok_sem, inc=1, device_id=along_y[d], device_id_type=MESH)

    def task(dz, dy, back=0):
        peer = {"grp": g, "wide": ((z + dz) % 4) * 4 + (y + dy) % 4}
        slot = tb.at[(y - dy) % 4, (z - dz) % 4] if back else tb.at[y, z]
        return remote(pack, slot, t_send.at[dz, dy], t_recv.at[dz, dy], peer)

    beside = [(dz, 0) for dz in (2, 1, 3)] + [(0, dy) for dy in (2, 1, 3)]
    beyond = [(dz, dy) for dz in (2, 1, 3) for dy in (2, 1, 3)]
    for dz, dy in beside:
        task(dz, dy).start()
    keep = pltpu.make_async_copy(pack, tb.at[y, z], t_send.at[0, 0])
    keep.start()

    hop = ((3, 0), (1, 1), (3, 1), (1, 0), (2, 0), (2, 1))

    def block(k, flip=0):
        return 2 * ((x + hop[k][0]) % 4) + (1 - s if flip else s)

    def rows(k, lo=0, n=128):
        return pl.ds(mine + hop[k][1] * 128 + lo, n)

    def x_own(h, k):
        r = rows(k)
        return remote(
            integ.at[0, r, pl.ds(h * 256, 256)],
            ib.at[h, own, r],
            x_send.at[h, k],
            x_recv.at[h, k],
            right if k in (0, 2) else left,
        )

    def x_relay(h, k):
        part = ib.at[h, block(k), rows(k)]
        return remote(
            part, part, x_send.at[h, k + 4], x_recv.at[h, k + 4], right if k == 0 else left
        )

    def x_in(h, k):
        part = ib.at[h, block(k), rows(k)]
        return remote(part, part, x_send.at[h, k], x_recv.at[h, k], right)

    def side_out(h, k, e):
        part = ib.at[h, block(k), rows(k, e * 64, 64)]
        return remote(
            part, part, q_send.at[h, k, e], q_recv.at[h, k, e], sides[hop[k][1] * 2 + e]
        )

    def side_in(h, k, e):
        part = ib.at[h, block(k), pl.ds(theirs + hop[k][1] * 128 + e * 64, 64)]
        return remote(part, part, q_send.at[h, k, e], q_recv.at[h, k, e], right)

    def twin_x(h, k, flip=0):
        part = ib.at[h, block(k, flip), rows(k)]
        return remote(part, part, c_send.at[h, 1 + k], c_recv.at[h, 1 + k], twin)

    first = (0, 1, 4)
    second = (2, 3, 5)

    def twin_q(h, j, flip=0):
        part = ib.at[h, block(first[j], flip), pl.ds(theirs, 256)]
        return remote(part, part, c_send.at[h, 7 + j], c_recv.at[h, 7 + j], twin)

    def twin_own(h):
        return remote(
            integ.at[0, :, pl.ds(h * 256, 256)],
            ib.at[h, own],
            c_send.at[h, 0],
            c_recv.at[h, 0],
            twin,
        )

    def twin_own_in(h):
        part = ib.at[h, 2 * x + 1 - s]
        return remote(part, part, c_send.at[h, 0], c_recv.at[h, 0], twin)

    def got_x(h, k):
        x_in(h, k).wait_recv()
        if k < 2:
            x_relay(h, k).start()
        side_out(h, k, 0).start()
        side_out(h, k, 1).start()
        twin_x(h, k).start()

    def got_q(h, j):
        for k in (first[j], second[j]):
            for e in range(2):
                side_in(h, k, e).wait_recv()
        twin_q(h, j).start()

    def got_twin(h, j):
        twin_x(h, first[j], 1).wait_recv()
        twin_x(h, second[j], 1).wait_recv()
        twin_q(h, j, 1).wait_recv()

    for h, k in ((0, 0), (0, 1), (0, 2), (0, 3), (1, 0), (1, 1)):
        x_own(h, k).start()
    for h in range(2):
        twin_own(h).start()
    pl.semaphore_wait(ok_sem, 3)
    for dz, dy in beyond:
        task(dz, dy).start()

    lane, row = iota((128, 128), 1), iota((128, 128), 0)

    def column(values, which):
        return jnp.sum(jnp.where(lane == which, values, 0.0), axis=1, keepdims=True)

    owner = column(pack[3:4, :].astype(f32), row % 16).astype(i32)
    sign_c = column((1 - 2 * (pack[5:6, :] & 1)).astype(f32), row // 16)
    sign_b = (1 - 2 * (pack[4:5, :] & 1)).astype(f32)[:, :32]
    which_c = row // 16
    local = iota((32, 128), 0) + w * 32
    real = iota((32, 128), 1) < 96

    keep.wait()
    got_x(0, 0)
    got_x(0, 1)
    for k in (2, 3):
        x_own(1, k).start()
    for dz, dy in beside + beyond:
        task(dz, dy, 1).wait_recv()
    hits, picks = [], []
    for v in range(16):
        names = tb[v // 4, v % 4]
        hits.append(
            jnp.where(
                (names[1:2, :] == which_c) & (names[2:3, :] == owner), 1.0, 0.0
            ).astype(bf16)
        )
        picks.append(
            jnp.where((names[0:1, :] == local) & real, 1.0, 0.0).astype(bf16)
        )
    t = lax.dot_general(
        jnp.concatenate(hits, axis=1),
        jnp.concatenate(picks, axis=1),
        (((1,), (1,)), ((), ())),
        preferred_element_type=f32,
    )
    t = (t * sign_b * sign_c).astype(bf16)
    spread = jnp.where(iota((32, 256), 0) == iota((32, 256), 1) // 8, 1.0, 0.0).astype(bf16)
    lift = jnp.where(iota((1024, 128), 1) == iota((1024, 128), 0) // 8, 1.0, 0.0).astype(bf16)
    wide_t = mm(lift, mm(t, spread).astype(bf16))
    tk[...] = jnp.where(
        iota((1024, 256), 0) % 8 == iota((1024, 256), 1) % 8, wide_t, 0.0
    ).astype(bf16)

    load.wait()

    def form(i, _):
        @pl.when(i == 1)
        def _():
            got_x(0, 2)
            got_x(0, 3)

        @pl.when(i == 4)
        def _():
            got_x(1, 0)
            got_x(1, 1)

        @pl.when(i == 6)
        def _():
            got_x(0, 4)
            got_x(0, 5)
            got_q(0, 0)
            got_q(0, 1)

        part = a_buf[:, pl.ds(pl.multiple_of(i * 8, 8), 8), :].reshape(256, 512)
        hi, lo = split(part)
        both = mm(tk[...], hi) + mm(tk[...], lo)
        hi, lo = split(both)
        shi[:, i] = hi.reshape(8, 128, 512)
        slo[:, i] = lo.reshape(8, 128, 512)
        return 0

    lax.fori_loop(0, 8, form, 0)

    every = pl.ds(0, 4)

    def part(h, a, f, e):
        if a == 0:
            return (h, slice(None), (z + f) % 4, e, slice(None), pl.ds(0, 128))
        return (h, slice(None), e, (y + f) % 4, slice(None), pl.ds(128, 128))

    def first_axis(a):
        return along_y if a else along_z

    def second_axis(a):
        return along_z if a else along_y

    def rs_first(h, a, d):
        return remote(
            acc.at[part(h, a, d, every)],
            near.at[h, a, d],
            n_send.at[h, a, d],
            n_recv.at[h, a, d],
            first_axis(a)[d],
        )

    def rs_last(h, a, d):
        to = (slice(None), ((z if a else y) + d) % 4)
        return remote(
            near.at[(h, a, 0) + to],
            fin.at[h, a, d],
            e_send.at[h, a, d],
            e_recv.at[h, a, d],
            second_axis(a)[d],
        )

    def rs_one(h):
        for d in (2, 1, 3):
            for a in range(2):
                rs_first(h, a, d).start()

    def rs_two(h):
        for a in range(2):
            for d in (1, 3, 2):
                rs_first(h, a, d).wait_recv()
            near[h, a, 0] = (
                near[h, a, 1] + near[h, a, 2] + near[h, a, 3] + acc[part(h, a, 0, every)]
            )
        for d in (2, 1, 3):
            for a in range(2):
                rs_last(h, a, d).start()

    def rs_end(h):
        for a in range(2):
            for d in (1, 3, 2):
                rs_last(h, a, d).wait_recv()
            cols = pl.ds(h * 256 + a * 128, 128)
            out[:, :, cols] = (
                base[:, :, cols]
                + near[h, a, 0, :, z if a else y]
                + fin[h, a, 1]
                + fin[h, a, 2]
                + fin[h, a, 3]
            )

    def events(u):
        if u == 0:
            loads[0].wait()
        if u == 1:
            twin_own_in(0).wait_recv()
            got_x(1, 2)
            got_x(1, 3)
        if u == 3:
            got_q(0, 2)
            got_twin(0, 0)
        if u == 4:
            got_x(1, 4)
            got_x(1, 5)
        if u == 5:
            got_twin(0, 1)
        if u == 6:
            got_q(1, 0)
            got_q(1, 1)
        if u == 7:
            got_twin(0, 2)
        if u == 8:
            rs_one(0)
            loads[1].wait()
        if u == 9:
            twin_own_in(1).wait_recv()
            got_q(1, 2)
        if u == 11:
            got_twin(1, 0)
        if u == 13:
            got_twin(1, 1)
        if u == 15:
            got_twin(1, 2)

    for u in range(16):
        events(u)
        h, v = u // 8, u % 8
        c = 2 * ((x + (0, 3, 1, 2)[v // 2]) % 4) + (1 - s if v % 2 else s)
        ihi, ilo = split(ib[h, c])
        for r in (slice(0, 4), slice(4, 8)):
            sh = shi[c, r].reshape(512, 512)
            sl = slo[c, r].reshape(512, 512)
            prod = (mm(sh, ihi) + mm(sh, ilo) + mm(sl, ihi)).reshape(4, 4, 4, 8, 256)
            acc[h, r] = prod if v == 0 else acc[h, r] + prod

    rs_one(1)
    rs_two(0)
    rs_two(1)
    rs_end(0)
    rs_end(1)

    for dz, dy in beside + beyond:
        task(dz, dy).wait_send()
    for h in range(2):
        for k in range(4):
            x_own(h, k).wait_send()
        for k in range(2):
            x_relay(h, k).wait_send()
        for k in range(6):
            side_out(h, k, 0).wait_send()
            side_out(h, k, 1).wait_send()
            twin_x(h, k).wait_send()
        for j in range(3):
            twin_q(h, j).wait_send()
        twin_own(h).wait_send()
        for a in range(2):
            for d in (1, 2, 3):
                rs_first(h, a, d).wait_send()
                rs_last(h, a, d).wait_send()


def fused(amplitudes, integrals, base, pack):
    vmem = pl.BlockSpec(memory_space=pltpu.VMEM)
    hbm = pl.BlockSpec(memory_space=pl.ANY)
    dma = pltpu.SemaphoreType.DMA
    return pl.pallas_call(
        kernel,
        out_shape=jax.ShapeDtypeStruct((8, 8, 512), f32),
        in_specs=[hbm, hbm, vmem, vmem],
        out_specs=vmem,
        scratch_shapes=[
            pltpu.VMEM((32, 64, 512), f32),
            pltpu.VMEM((2, 8, 512, 256), f32),
            pltpu.VMEM((8, 8, 128, 512), bf16),
            pltpu.VMEM((8, 8, 128, 512), bf16),
            pltpu.VMEM((1024, 256), bf16),
            pltpu.VMEM((2, 8, 4, 4, 8, 256), f32),
            pltpu.VMEM((4, 4, 8, 128), i32),
            pltpu.VMEM((2, 2, 4, 8, 4, 8, 128), f32),
            pltpu.VMEM((2, 2, 4, 8, 8, 128), f32),
            dma,
            dma((2,)),
            dma((4, 4)),
            dma((4, 4)),
            dma((2, 6)),
            dma((2, 6)),
            dma((2, 6, 2)),
            dma((2, 6, 2)),
            dma((2, 10)),
            dma((2, 10)),
            dma((2, 2, 4)),
            dma((2, 2, 4)),
            dma((2, 2, 4)),
            dma((2, 2, 4)),
            pltpu.SemaphoreType.REGULAR,
        ],
        compiler_params=pltpu.CompilerParams(
            collective_id=0, has_side_effects=True, vmem_limit_bytes=60 * 2**20
        ),
    )(amplitudes, integrals, base, pack)


def line(values, row):
    values = values.reshape(1, -1)
    return jnp.pad(values, ((row, 7 - row), (0, 128 - values.shape[1])))


def on_device(
    amplitudes,
    integrals,
    base_residual,
    occ_gap,
    virt_sum,
    task_amp,
    task_int,
    task_res,
    task_count,
    res_owner,
    amp_label,
    int_label,
):
    used = jnp.arange(96, dtype=i32)[None] < task_count[0]
    pack = (
        line(jnp.where(used, task_amp, -1), 0)
        + line(task_int, 1)
        + line(task_res, 2)
        + line(res_owner, 3)
        + line(amp_label, 4)
        + line(int_label, 5)
    )
    summed = fused(amplitudes, integrals, base_residual.reshape(8, 8, 512), pack)
    divisor = occ_gap[:, :, None] + virt_sum[None, None, :]
    return summed.reshape(1, 64, 512) / divisor


def solution(mesh):
    both = ("grp", "wide")
    return jax.shard_map(
        on_device,
        mesh=mesh,
        in_specs=(
            P(both, None, None),
            P("grp", None, None),
            P(both, None, None),
            P(both, None),
            P(),
            P(both, None),
            P(both, None),
            P(both, None),
            P(both),
            P("grp", None),
            P(both),
            P(),
        ),
        out_specs=P(both, None, None),
        check_vma=False,
    )
```

```python
import jax
import jax.numpy as jnp
from jax import lax
from jax.experimental import pallas as pl
from jax.experimental.pallas import tpu as pltpu
from jax.sharding import PartitionSpec as P

MESH = pl.DeviceIdType.MESH
f32, bf16, i32 = jnp.float32, jnp.bfloat16, jnp.int32


def iota(shape, dim):
    return lax.broadcasted_iota(i32, shape, dim)


def split(v):
    hi = v.astype(bf16)
    return hi, (v - hi.astype(f32)).astype(bf16)


def mm(a, b):
    return jnp.dot(a, b, preferred_element_type=f32)


def kernel(
    amp,
    integ,
    base,
    gap,
    virt,
    amp_ids,
    int_ids,
    res_ids,
    count,
    owners,
    amp_label,
    int_label,
    out,
    pack,
    a_buf,
    ib,
    shi,
    slo,
    tk,
    acc,
    tb,
    near,
    fin,
    a_sem,
    own_sem,
    t_send,
    t_recv,
    x_send,
    x_recv,
    q_send,
    q_recv,
    c_send,
    c_recv,
    n_send,
    n_recv,
    e_send,
    e_recv,
    ok_sem,
):
    g = lax.axis_index("grp")
    w = lax.axis_index("wide")
    x, s = g // 2, g % 2
    z, y = w // 4, w % 4
    par = (y + z) % 2
    right = {"grp": ((x + 1) % 4) * 2 + s, "wide": w}
    left = {"grp": ((x + 3) % 4) * 2 + s, "wide": w}
    twin = {"grp": x * 2 + 1 - s, "wide": w}
    sides = (
        {"grp": g, "wide": z * 4 + (y + 1) % 4},
        {"grp": g, "wide": z * 4 + (y + 3) % 4},
        {"grp": g, "wide": ((z + 1) % 4) * 4 + y},
        {"grp": g, "wide": ((z + 3) % 4) * 4 + y},
    )
    mine = par * 256
    theirs = (1 - par) * 256
    own = g
    along_z = [{"grp": g, "wide": ((z + d) % 4) * 4 + y} for d in range(4)]
    along_y = [{"grp": g, "wide": z * 4 + (y + d) % 4} for d in range(4)]

    def remote(src, dst, send, recv, dev):
        return pltpu.make_async_remote_copy(
            src_ref=src,
            dst_ref=dst,
            send_sem=send,
            recv_sem=recv,
            device_id=dev,
            device_id_type=MESH,
        )

    load = pltpu.make_async_copy(amp, a_buf, a_sem)
    load.start()
    loads = []
    for h in range(2):
        loads.append(
            pltpu.make_async_copy(
                integ.at[0, :, pl.ds(h * 256, 256)], ib.at[h, own], own_sem.at[h]
            )
        )
        loads[h].start()

    pack[...] = jnp.zeros_like(pack)
    used = iota((1, 96), 1) < count[0]
    pack[0:1, 0:96] = jnp.where(used, amp_ids[...], -1)
    pack[1:2, 0:96] = int_ids[...]
    pack[2:3, 0:96] = res_ids[...]

    barrier = pltpu.get_barrier_semaphore()
    for dev in (right, left, twin, *along_z[1:], *along_y[1:]):
        pl.semaphore_signal(barrier, inc=1, device_id=dev, device_id_type=MESH)
    pl.semaphore_wait(barrier, 9)

    for d in range(1, 4):
        pl.semaphore_signal(ok_sem, inc=1, device_id=along_y[d], device_id_type=MESH)

    def task(dz, dy, back=0):
        peer = {"grp": g, "wide": ((z + dz) % 4) * 4 + (y + dy) % 4}
        slot = tb.at[(y - dy) % 4, (z - dz) % 4] if back else tb.at[y, z]
        return remote(pack, slot, t_send.at[dz, dy], t_recv.at[dz, dy], peer)

    beside = [(dz, 0) for dz in (2, 1, 3)] + [(0, dy) for dy in (2, 1, 3)]
    beyond = [(dz, dy) for dz in (2, 1, 3) for dy in (2, 1, 3)]
    for dz, dy in beside:
        task(dz, dy).start()
    keep = pltpu.make_async_copy(pack, tb.at[y, z], t_send.at[0, 0])
    keep.start()

    hop = ((3, 0), (1, 1), (3, 1), (1, 0), (2, 0), (2, 1))

    def block(k, flip=0):
        return 2 * ((x + hop[k][0]) % 4) + (1 - s if flip else s)

    def rows(k, lo=0, n=128):
        return pl.ds(mine + hop[k][1] * 128 + lo, n)

    def x_own(h, k):
        r = rows(k)
        return remote(
            integ.at[0, r, pl.ds(h * 256, 256)],
            ib.at[h, own, r],
            x_send.at[h, k],
            x_recv.at[h, k],
            right if k in (0, 2) else left,
        )

    def x_relay(h, k):
        part = ib.at[h, block(k), rows(k)]
        return remote(
            part, part, x_send.at[h, k + 4], x_recv.at[h, k + 4], right if k == 0 else left
        )

    def x_in(h, k):
        part = ib.at[h, block(k), rows(k)]
        return remote(part, part, x_send.at[h, k], x_recv.at[h, k], right)

    def side_out(h, k, e):
        part = ib.at[h, block(k), rows(k, e * 64, 64)]
        return remote(
            part, part, q_send.at[h, k, e], q_recv.at[h, k, e], sides[hop[k][1] * 2 + e]
        )

    def side_in(h, k, e):
        part = ib.at[h, block(k), pl.ds(theirs + hop[k][1] * 128 + e * 64, 64)]
        return remote(part, part, q_send.at[h, k, e], q_recv.at[h, k, e], right)

    def twin_x(h, k, flip=0):
        part = ib.at[h, block(k, flip), rows(k)]
        return remote(part, part, c_send.at[h, 1 + k], c_recv.at[h, 1 + k], twin)

    first = (0, 1, 4)
    second = (2, 3, 5)

    def twin_q(h, j, flip=0):
        part = ib.at[h, block(first[j], flip), pl.ds(theirs, 256)]
        return remote(part, part, c_send.at[h, 7 + j], c_recv.at[h, 7 + j], twin)

    def twin_own(h):
        return remote(
            integ.at[0, :, pl.ds(h * 256, 256)],
            ib.at[h, own],
            c_send.at[h, 0],
            c_recv.at[h, 0],
            twin,
        )

    def twin_own_in(h):
        part = ib.at[h, 2 * x + 1 - s]
        return remote(part, part, c_send.at[h, 0], c_recv.at[h, 0], twin)

    def got_x(h, k):
        x_in(h, k).wait_recv()
        if k < 2:
            x_relay(h, k).start()
        side_out(h, k, 0).start()
        side_out(h, k, 1).start()
        twin_x(h, k).start()

    def got_q(h, j):
        for k in (first[j], second[j]):
            for e in range(2):
                side_in(h, k, e).wait_recv()
        twin_q(h, j).start()

    def got_twin(h, j):
        twin_x(h, first[j], 1).wait_recv()
        twin_x(h, second[j], 1).wait_recv()
        twin_q(h, j, 1).wait_recv()

    for h, k in ((0, 0), (0, 1), (0, 2), (0, 3), (1, 0), (1, 1)):
        x_own(h, k).start()
    for h in range(2):
        twin_own(h).start()
    pl.semaphore_wait(ok_sem, 3)
    for dz, dy in beyond:
        task(dz, dy).start()

    row = iota((128, 128), 0)

    def column(values, n, which):
        lanes = iota((n, values.shape[1]), 1)
        return jnp.sum(jnp.where(lanes == which, values, 0.0), axis=1, keepdims=True)

    place = iota((128, 1), 0)
    owner = column(owners[...].astype(f32), 128, place % 16).astype(i32)
    sign_c = column((1 - 2 * (int_label[...] & 1)).astype(f32), 128, place // 16)
    sign_b = (1 - 2 * (amp_label[...] & 1)).astype(f32)
    which_c = row // 16
    gaps = column(gap[...], 64, iota((64, 1), 0)).reshape(8, 8, 1)
    local = iota((32, 128), 0) + w * 32
    real = iota((32, 128), 1) < 96

    keep.wait()
    got_x(0, 0)
    got_x(0, 1)
    for k in (2, 3):
        x_own(1, k).start()
    for dz, dy in beside + beyond:
        task(dz, dy, 1).wait_recv()
    hits, picks = [], []
    for v in range(16):
        names = tb[v // 4, v % 4]
        hits.append(
            jnp.where(
                (names[1:2, :] == which_c) & (names[2:3, :] == owner), 1.0, 0.0
            ).astype(bf16)
        )
        picks.append(
            jnp.where((names[0:1, :] == local) & real, 1.0, 0.0).astype(bf16)
        )
    t = lax.dot_general(
        jnp.concatenate(hits, axis=1),
        jnp.concatenate(picks, axis=1),
        (((1,), (1,)), ((), ())),
        preferred_element_type=f32,
    )
    t = (t * sign_b * sign_c).astype(bf16)
    spread = jnp.where(iota((32, 256), 0) == iota((32, 256), 1) // 8, 1.0, 0.0).astype(bf16)
    lift = jnp.where(iota((1024, 128), 1) == iota((1024, 128), 0) // 8, 1.0, 0.0).astype(bf16)
    wide_t = mm(lift, mm(t, spread).astype(bf16))
    tk[...] = jnp.where(
        iota((1024, 256), 0) % 8 == iota((1024, 256), 1) % 8, wide_t, 0.0
    ).astype(bf16)

    load.wait()

    def form(i, _):
        @pl.when(i == 1)
        def _():
            got_x(0, 2)
            got_x(0, 3)

        @pl.when(i == 4)
        def _():
            got_x(1, 0)
            got_x(1, 1)

        @pl.when(i == 6)
        def _():
            got_x(0, 4)
            got_x(0, 5)
            got_q(0, 0)
            got_q(0, 1)

        part = a_buf[:, pl.ds(pl.multiple_of(i * 8, 8), 8), :].reshape(256, 512)
        hi, lo = split(part)
        both = mm(tk[...], hi) + mm(tk[...], lo)
        hi, lo = split(both)
        shi[:, i] = hi.reshape(8, 128, 512)
        slo[:, i] = lo.reshape(8, 128, 512)
        return 0

    lax.fori_loop(0, 8, form, 0)

    every = pl.ds(0, 4)

    def part(h, a, f, e):
        if a == 0:
            return (h, slice(None), (z + f) % 4, e, slice(None), pl.ds(0, 128))
        return (h, slice(None), e, (y + f) % 4, slice(None), pl.ds(128, 128))

    def first_axis(a):
        return along_y if a else along_z

    def second_axis(a):
        return along_z if a else along_y

    def rs_first(h, a, d):
        return remote(
            acc.at[part(h, a, d, every)],
            near.at[h, a, d],
            n_send.at[h, a, d],
            n_recv.at[h, a, d],
            first_axis(a)[d],
        )

    def rs_last(h, a, d):
        to = (slice(None), ((z if a else y) + d) % 4)
        return remote(
            near.at[(h, a, 0) + to],
            fin.at[h, a, d],
            e_send.at[h, a, d],
            e_recv.at[h, a, d],
            second_axis(a)[d],
        )

    def rs_one(h):
        for d in (2, 1, 3):
            for a in range(2):
                rs_first(h, a, d).start()

    def rs_two(h):
        for a in range(2):
            for d in (1, 3, 2):
                rs_first(h, a, d).wait_recv()
            near[h, a, 0] = (
                near[h, a, 1] + near[h, a, 2] + near[h, a, 3] + acc[part(h, a, 0, every)]
            )
        for d in (2, 1, 3):
            for a in range(2):
                rs_last(h, a, d).start()

    def rs_end(h):
        for a in range(2):
            for d in (1, 3, 2):
                rs_last(h, a, d).wait_recv()
            cols = pl.ds(h * 256 + a * 128, 128)
            out[:, :, cols] = (
                base[:, :, cols]
                + near[h, a, 0, :, z if a else y]
                + fin[h, a, 1]
                + fin[h, a, 2]
                + fin[h, a, 3]
            ) / (gaps + virt[:, cols].reshape(1, 1, 128))

    def events(u):
        if u == 0:
            loads[0].wait()
        if u == 1:
            twin_own_in(0).wait_recv()
            got_x(1, 2)
            got_x(1, 3)
        if u == 3:
            got_q(0, 2)
            got_twin(0, 0)
        if u == 4:
            got_x(1, 4)
            got_x(1, 5)
        if u == 5:
            got_twin(0, 1)
        if u == 6:
            got_q(1, 0)
            got_q(1, 1)
        if u == 7:
            got_twin(0, 2)
        if u == 8:
            rs_one(0)
            loads[1].wait()
        if u == 9:
            twin_own_in(1).wait_recv()
            got_q(1, 2)
        if u == 11:
            got_twin(1, 0)
        if u == 13:
            got_twin(1, 1)
        if u == 15:
            got_twin(1, 2)

    for u in range(16):
        events(u)
        h, v = u // 8, u % 8
        c = 2 * ((x + (0, 3, 1, 2)[v // 2]) % 4) + (1 - s if v % 2 else s)
        ihi, ilo = split(ib[h, c])
        for r in (slice(0, 4), slice(4, 8)):
            sh = shi[c, r].reshape(512, 512)
            sl = slo[c, r].reshape(512, 512)
            prod = (mm(sh, ihi) + mm(sh, ilo) + mm(sl, ihi)).reshape(4, 4, 4, 8, 256)
            acc[h, r] = prod if v == 0 else acc[h, r] + prod

    rs_one(1)
    rs_two(0)
    rs_two(1)
    rs_end(0)
    rs_end(1)

    for dz, dy in beside + beyond:
        task(dz, dy).wait_send()
    for h in range(2):
        for k in range(4):
            x_own(h, k).wait_send()
        for k in range(2):
            x_relay(h, k).wait_send()
        for k in range(6):
            side_out(h, k, 0).wait_send()
            side_out(h, k, 1).wait_send()
            twin_x(h, k).wait_send()
        for j in range(3):
            twin_q(h, j).wait_send()
        twin_own(h).wait_send()
        for a in range(2):
            for d in (1, 2, 3):
                rs_first(h, a, d).wait_send()
                rs_last(h, a, d).wait_send()


def fused(amplitudes, integrals, base, *small):
    vmem = pl.BlockSpec(memory_space=pltpu.VMEM)
    hbm = pl.BlockSpec(memory_space=pl.ANY)
    smem = pl.BlockSpec(memory_space=pltpu.SMEM)
    dma = pltpu.SemaphoreType.DMA
    return pl.pallas_call(
        kernel,
        out_shape=jax.ShapeDtypeStruct((8, 8, 512), f32),
        in_specs=[hbm, hbm, *[vmem] * 6, smem, *[vmem] * 3],
        out_specs=vmem,
        scratch_shapes=[
            pltpu.VMEM((8, 128), i32),
            pltpu.VMEM((32, 64, 512), f32),
            pltpu.VMEM((2, 8, 512, 256), f32),
            pltpu.VMEM((8, 8, 128, 512), bf16),
            pltpu.VMEM((8, 8, 128, 512), bf16),
            pltpu.VMEM((1024, 256), bf16),
            pltpu.VMEM((2, 8, 4, 4, 8, 256), f32),
            pltpu.VMEM((4, 4, 8, 128), i32),
            pltpu.VMEM((2, 2, 4, 8, 4, 8, 128), f32),
            pltpu.VMEM((2, 2, 4, 8, 8, 128), f32),
            dma,
            dma((2,)),
            dma((4, 4)),
            dma((4, 4)),
            dma((2, 6)),
            dma((2, 6)),
            dma((2, 6, 2)),
            dma((2, 6, 2)),
            dma((2, 10)),
            dma((2, 10)),
            dma((2, 2, 4)),
            dma((2, 2, 4)),
            dma((2, 2, 4)),
            dma((2, 2, 4)),
            pltpu.SemaphoreType.REGULAR,
        ],
        compiler_params=pltpu.CompilerParams(
            collective_id=0, has_side_effects=True, vmem_limit_bytes=60 * 2**20
        ),
    )(amplitudes, integrals, base, *small)


def on_device(
    amplitudes,
    integrals,
    base_residual,
    occ_gap,
    virt_sum,
    task_amp,
    task_int,
    task_res,
    task_count,
    res_owner,
    amp_label,
    int_label,
):
    out = fused(
        amplitudes,
        integrals,
        base_residual.reshape(8, 8, 512),
        occ_gap,
        virt_sum.reshape(1, 512),
        task_amp,
        task_int,
        task_res,
        task_count,
        res_owner,
        amp_label.reshape(1, 32),
        int_label.reshape(1, 8),
    )
    return out.reshape(1, 64, 512)


def solution(mesh):
    both = ("grp", "wide")
    return jax.shard_map(
        on_device,
        mesh=mesh,
        in_specs=(
            P(both, None, None),
            P("grp", None, None),
            P(both, None, None),
            P(both, None),
            P(),
            P(both, None),
            P(both, None),
            P(both, None),
            P(both),
            P("grp", None),
            P(both),
            P(),
        ),
        out_specs=P(both, None, None),
        check_vma=False,
    )
```

```python
import jax
import jax.numpy as jnp
from jax import lax
from jax.experimental import pallas as pl
from jax.experimental.pallas import tpu as pltpu
from jax.sharding import PartitionSpec as P

MESH = pl.DeviceIdType.MESH
f32, bf16, i32 = jnp.float32, jnp.bfloat16, jnp.int32


def iota(shape, dim):
    return lax.broadcasted_iota(i32, shape, dim)


def split(v):
    hi = v.astype(bf16)
    return hi, (v - hi.astype(f32)).astype(bf16)


def mm(a, b):
    return jnp.dot(a, b, preferred_element_type=f32)


def kernel(
    amp,
    integ,
    base,
    gap,
    virt,
    amp_ids,
    int_ids,
    res_ids,
    count,
    owners,
    amp_label,
    int_label,
    out,
    pack,
    a_buf,
    ib,
    shi,
    slo,
    tk,
    acc,
    tb,
    near,
    fin,
    a_sem,
    own_sem,
    t_send,
    t_recv,
    x_send,
    x_recv,
    q_send,
    q_recv,
    c_send,
    c_recv,
    n_send,
    n_recv,
    e_send,
    e_recv,
    ok_sem,
):
    g = lax.axis_index("grp")
    w = lax.axis_index("wide")
    x, s = g // 2, g % 2
    z, y = w // 4, w % 4
    par = (y + z) % 2
    right = {"grp": ((x + 1) % 4) * 2 + s, "wide": w}
    left = {"grp": ((x + 3) % 4) * 2 + s, "wide": w}
    twin = {"grp": x * 2 + 1 - s, "wide": w}
    sides = (
        {"grp": g, "wide": z * 4 + (y + 1) % 4},
        {"grp": g, "wide": z * 4 + (y + 3) % 4},
        {"grp": g, "wide": ((z + 1) % 4) * 4 + y},
        {"grp": g, "wide": ((z + 3) % 4) * 4 + y},
    )
    mine = par * 256
    theirs = (1 - par) * 256
    own = g
    along_z = [{"grp": g, "wide": ((z + d) % 4) * 4 + y} for d in range(4)]
    along_y = [{"grp": g, "wide": z * 4 + (y + d) % 4} for d in range(4)]

    def remote(src, dst, send, recv, dev):
        return pltpu.make_async_remote_copy(
            src_ref=src,
            dst_ref=dst,
            send_sem=send,
            recv_sem=recv,
            device_id=dev,
            device_id_type=MESH,
        )

    load = pltpu.make_async_copy(amp, a_buf, a_sem)
    load.start()
    loads = []
    for h in range(2):
        loads.append(
            pltpu.make_async_copy(
                integ.at[0, :, pl.ds(h * 256, 256)], ib.at[h, own], own_sem.at[h]
            )
        )
        loads[h].start()

    pack[...] = jnp.zeros_like(pack)
    used = iota((1, 96), 1) < count[0]
    pack[0:1, 0:96] = jnp.where(used, amp_ids[...], -1)
    pack[1:2, 0:96] = int_ids[...]
    pack[2:3, 0:96] = res_ids[...]

    barrier = pltpu.get_barrier_semaphore()
    for dev in (right, left, twin, *along_z[1:], *along_y[1:]):
        pl.semaphore_signal(barrier, inc=1, device_id=dev, device_id_type=MESH)
    pl.semaphore_wait(barrier, 9)

    for d in range(1, 4):
        pl.semaphore_signal(ok_sem, inc=1, device_id=along_y[d], device_id_type=MESH)

    def task(dz, dy, back=0):
        peer = {"grp": g, "wide": ((z + dz) % 4) * 4 + (y + dy) % 4}
        slot = tb.at[(y - dy) % 4, (z - dz) % 4] if back else tb.at[y, z]
        return remote(pack, slot, t_send.at[dz, dy], t_recv.at[dz, dy], peer)

    beside = [(dz, 0) for dz in (2, 1, 3)] + [(0, dy) for dy in (2, 1, 3)]
    beyond = [(dz, dy) for dz in (2, 1, 3) for dy in (2, 1, 3)]
    for dz, dy in beside:
        task(dz, dy).start()
    keep = pltpu.make_async_copy(pack, tb.at[y, z], t_send.at[0, 0])
    keep.start()

    hop = ((3, 0), (1, 1), (3, 1), (1, 0), (2, 0), (2, 1))

    def block(k, flip=0):
        return 2 * ((x + hop[k][0]) % 4) + (1 - s if flip else s)

    def rows(k, lo=0, n=128):
        return pl.ds(mine + hop[k][1] * 128 + lo, n)

    def x_own(h, k):
        r = rows(k)
        return remote(
            integ.at[0, r, pl.ds(h * 256, 256)],
            ib.at[h, own, r],
            x_send.at[h, k],
            x_recv.at[h, k],
            right if k in (0, 2) else left,
        )

    def x_relay(h, k):
        part = ib.at[h, block(k), rows(k)]
        return remote(
            part, part, x_send.at[h, k + 4], x_recv.at[h, k + 4], right if k == 0 else left
        )

    def x_in(h, k):
        part = ib.at[h, block(k), rows(k)]
        return remote(part, part, x_send.at[h, k], x_recv.at[h, k], right)

    def side_out(h, k, e):
        part = ib.at[h, block(k), rows(k, e * 64, 64)]
        return remote(
            part, part, q_send.at[h, k, e], q_recv.at[h, k, e], sides[hop[k][1] * 2 + e]
        )

    def side_in(h, k, e):
        part = ib.at[h, block(k), pl.ds(theirs + hop[k][1] * 128 + e * 64, 64)]
        return remote(part, part, q_send.at[h, k, e], q_recv.at[h, k, e], right)

    def twin_x(h, k, flip=0):
        part = ib.at[h, block(k, flip), rows(k)]
        return remote(part, part, c_send.at[h, 1 + k], c_recv.at[h, 1 + k], twin)

    first = (0, 1, 4)
    second = (2, 3, 5)

    def twin_q(h, j, flip=0):
        part = ib.at[h, block(first[j], flip), pl.ds(theirs, 256)]
        return remote(part, part, c_send.at[h, 7 + j], c_recv.at[h, 7 + j], twin)

    def twin_own(h):
        return remote(
            integ.at[0, :, pl.ds(h * 256, 256)],
            ib.at[h, own],
            c_send.at[h, 0],
            c_recv.at[h, 0],
            twin,
        )

    def twin_own_in(h):
        part = ib.at[h, 2 * x + 1 - s]
        return remote(part, part, c_send.at[h, 0], c_recv.at[h, 0], twin)

    def got_x(h, k):
        x_in(h, k).wait_recv()
        if k < 2:
            x_relay(h, k).start()
        side_out(h, k, 0).start()
        side_out(h, k, 1).start()
        twin_x(h, k).start()

    def got_q(h, j):
        for k in (first[j], second[j]):
            for e in range(2):
                side_in(h, k, e).wait_recv()
        twin_q(h, j).start()

    def got_twin(h, j):
        twin_x(h, first[j], 1).wait_recv()
        twin_x(h, second[j], 1).wait_recv()
        twin_q(h, j, 1).wait_recv()

    for h, k in ((0, 0), (0, 1), (0, 2), (0, 3), (1, 0), (1, 1)):
        x_own(h, k).start()
    for h in range(2):
        twin_own(h).start()
    pl.semaphore_wait(ok_sem, 3)
    for dz, dy in beyond:
        task(dz, dy).start()

    row = iota((128, 128), 0)

    def column(values, n, which):
        lanes = iota((n, values.shape[1]), 1)
        return jnp.sum(jnp.where(lanes == which, values, 0.0), axis=1, keepdims=True)

    place = iota((128, 1), 0)
    owner = column(owners[...].astype(f32), 128, place % 16).astype(i32)
    sign_c = column((1 - 2 * (int_label[...] & 1)).astype(f32), 128, place // 16)
    sign_b = (1 - 2 * (amp_label[...] & 1)).astype(f32)
    which_c = row // 16
    gaps = column(gap[...], 64, iota((64, 1), 0)).reshape(8, 8, 1)
    local = iota((32, 128), 0) + w * 32
    real = iota((32, 128), 1) < 96

    keep.wait()
    got_x(0, 0)
    got_x(0, 1)
    for k in (2, 3):
        x_own(1, k).start()
    for dz, dy in beside + beyond:
        task(dz, dy, 1).wait_recv()
    hits, picks = [], []
    for v in range(16):
        names = tb[v // 4, v % 4]
        hits.append(
            jnp.where(
                (names[1:2, :] == which_c) & (names[2:3, :] == owner), 1.0, 0.0
            ).astype(bf16)
        )
        picks.append(
            jnp.where((names[0:1, :] == local) & real, 1.0, 0.0).astype(bf16)
        )
    t = lax.dot_general(
        jnp.concatenate(hits, axis=1),
        jnp.concatenate(picks, axis=1),
        (((1,), (1,)), ((), ())),
        preferred_element_type=f32,
    )
    t = (t * sign_b * sign_c).astype(bf16)
    spread = jnp.where(iota((32, 256), 0) == iota((32, 256), 1) // 8, 1.0, 0.0).astype(bf16)
    lift = jnp.where(iota((1024, 128), 1) == iota((1024, 128), 0) // 8, 1.0, 0.0).astype(bf16)
    wide_t = mm(lift, mm(t, spread).astype(bf16))
    tk[...] = jnp.where(
        iota((1024, 256), 0) % 8 == iota((1024, 256), 1) % 8, wide_t, 0.0
    ).astype(bf16)

    load.wait()

    def form(i, _):
        @pl.when(i == 2)
        def _():
            got_x(0, 2)
            got_x(0, 3)

        @pl.when(i == 5)
        def _():
            got_x(1, 0)
            got_x(1, 1)

        part = a_buf[:, pl.ds(pl.multiple_of(i * 8, 8), 8), :].reshape(256, 512)
        hi, lo = split(part)
        both = mm(tk[...], hi) + mm(tk[...], lo)
        hi, lo = split(both)
        shi[:, i] = hi.reshape(8, 128, 512)
        slo[:, i] = lo.reshape(8, 128, 512)
        return 0

    lax.fori_loop(0, 8, form, 0)

    every = pl.ds(0, 4)

    def part(h, a, f, e):
        if a == 0:
            return (h, slice(None), (z + f) % 4, e, slice(None), pl.ds(0, 128))
        return (h, slice(None), e, (y + f) % 4, slice(None), pl.ds(128, 128))

    def first_axis(a):
        return along_y if a else along_z

    def second_axis(a):
        return along_z if a else along_y

    def rs_first(h, a, d):
        return remote(
            acc.at[part(h, a, d, every)],
            near.at[h, a, d],
            n_send.at[h, a, d],
            n_recv.at[h, a, d],
            first_axis(a)[d],
        )

    def rs_last(h, a, d):
        to = (slice(None), ((z if a else y) + d) % 4)
        return remote(
            near.at[(h, a, 0) + to],
            fin.at[h, a, d],
            e_send.at[h, a, d],
            e_recv.at[h, a, d],
            second_axis(a)[d],
        )

    def rs_one(h):
        for d in (2, 1, 3):
            for a in range(2):
                rs_first(h, a, d).start()

    def rs_two(h):
        for a in range(2):
            for d in (1, 3, 2):
                rs_first(h, a, d).wait_recv()
            near[h, a, 0] = (
                near[h, a, 1] + near[h, a, 2] + near[h, a, 3] + acc[part(h, a, 0, every)]
            )
        for d in (2, 1, 3):
            for a in range(2):
                rs_last(h, a, d).start()

    def rs_end(h):
        for a in range(2):
            for d in (1, 3, 2):
                rs_last(h, a, d).wait_recv()
            cols = pl.ds(h * 256 + a * 128, 128)
            out[:, :, cols] = (
                base[:, :, cols]
                + near[h, a, 0, :, z if a else y]
                + fin[h, a, 1]
                + fin[h, a, 2]
                + fin[h, a, 3]
            ) / (gaps + virt[:, cols].reshape(1, 1, 128))

    def events(u):
        if u == 0:
            loads[0].wait()
            got_x(0, 4)
            got_x(0, 5)
        if u == 1:
            twin_own_in(0).wait_recv()
            got_q(0, 0)
            got_q(0, 1)
        if u == 2:
            loads[1].wait()
            got_x(1, 2)
            got_x(1, 3)
        if u == 3:
            twin_own_in(1).wait_recv()
        if u == 4:
            got_q(0, 2)
        if u == 5:
            got_twin(0, 0)
            got_x(1, 4)
            got_x(1, 5)
        if u == 7:
            got_twin(0, 1)
            got_q(1, 0)
            got_q(1, 1)
        if u == 9:
            got_twin(0, 2)
        if u == 10:
            rs_one(0)
            got_q(1, 2)
        if u == 11:
            got_twin(1, 0)
        if u == 13:
            got_twin(1, 1)
        if u == 15:
            got_twin(1, 2)

    order = [(h, v) for h in range(2) for v in range(2)]
    order += [(h, v) for h in range(2) for v in range(2, 8)]
    for u, (h, v) in enumerate(order):
        events(u)
        c = 2 * ((x + (0, 3, 1, 2)[v // 2]) % 4) + (1 - s if v % 2 else s)
        ihi, ilo = split(ib[h, c])
        for r in (slice(0, 4), slice(4, 8)):
            sh = shi[c, r].reshape(512, 512)
            sl = slo[c, r].reshape(512, 512)
            prod = (mm(sh, ihi) + mm(sh, ilo) + mm(sl, ihi)).reshape(4, 4, 4, 8, 256)
            acc[h, r] = prod if v == 0 else acc[h, r] + prod

    rs_one(1)
    rs_two(0)
    rs_two(1)
    rs_end(0)
    rs_end(1)

    for dz, dy in beside + beyond:
        task(dz, dy).wait_send()
    for h in range(2):
        for k in range(4):
            x_own(h, k).wait_send()
        for k in range(2):
            x_relay(h, k).wait_send()
        for k in range(6):
            side_out(h, k, 0).wait_send()
            side_out(h, k, 1).wait_send()
            twin_x(h, k).wait_send()
        for j in range(3):
            twin_q(h, j).wait_send()
        twin_own(h).wait_send()
        for a in range(2):
            for d in (1, 2, 3):
                rs_first(h, a, d).wait_send()
                rs_last(h, a, d).wait_send()


def fused(amplitudes, integrals, base, *small):
    vmem = pl.BlockSpec(memory_space=pltpu.VMEM)
    hbm = pl.BlockSpec(memory_space=pl.ANY)
    smem = pl.BlockSpec(memory_space=pltpu.SMEM)
    dma = pltpu.SemaphoreType.DMA
    return pl.pallas_call(
        kernel,
        out_shape=jax.ShapeDtypeStruct((8, 8, 512), f32),
        in_specs=[hbm, hbm, *[vmem] * 6, smem, *[vmem] * 3],
        out_specs=vmem,
        scratch_shapes=[
            pltpu.VMEM((8, 128), i32),
            pltpu.VMEM((32, 64, 512), f32),
            pltpu.VMEM((2, 8, 512, 256), f32),
            pltpu.VMEM((8, 8, 128, 512), bf16),
            pltpu.VMEM((8, 8, 128, 512), bf16),
            pltpu.VMEM((1024, 256), bf16),
            pltpu.VMEM((2, 8, 4, 4, 8, 256), f32),
            pltpu.VMEM((4, 4, 8, 128), i32),
            pltpu.VMEM((2, 2, 4, 8, 4, 8, 128), f32),
            pltpu.VMEM((2, 2, 4, 8, 8, 128), f32),
            dma,
            dma((2,)),
            dma((4, 4)),
            dma((4, 4)),
            dma((2, 6)),
            dma((2, 6)),
            dma((2, 6, 2)),
            dma((2, 6, 2)),
            dma((2, 10)),
            dma((2, 10)),
            dma((2, 2, 4)),
            dma((2, 2, 4)),
            dma((2, 2, 4)),
            dma((2, 2, 4)),
            pltpu.SemaphoreType.REGULAR,
        ],
        compiler_params=pltpu.CompilerParams(
            collective_id=0, has_side_effects=True, vmem_limit_bytes=60 * 2**20
        ),
    )(amplitudes, integrals, base, *small)


def on_device(
    amplitudes,
    integrals,
    base_residual,
    occ_gap,
    virt_sum,
    task_amp,
    task_int,
    task_res,
    task_count,
    res_owner,
    amp_label,
    int_label,
):
    out = fused(
        amplitudes,
        integrals,
        base_residual.reshape(8, 8, 512),
        occ_gap,
        virt_sum.reshape(1, 512),
        task_amp,
        task_int,
        task_res,
        task_count,
        res_owner,
        amp_label.reshape(1, 32),
        int_label.reshape(1, 8),
    )
    return out.reshape(1, 64, 512)


def solution(mesh):
    both = ("grp", "wide")
    return jax.shard_map(
        on_device,
        mesh=mesh,
        in_specs=(
            P(both, None, None),
            P("grp", None, None),
            P(both, None, None),
            P(both, None),
            P(),
            P(both, None),
            P(both, None),
            P(both, None),
            P(both),
            P("grp", None),
            P(both),
            P(),
        ),
        out_specs=P(both, None, None),
        check_vma=False,
    )
```

```python
import jax
import jax.numpy as jnp
from jax import lax
from jax.experimental import pallas as pl
from jax.experimental.pallas import tpu as pltpu
from jax.sharding import PartitionSpec as P

MESH = pl.DeviceIdType.MESH
f32, bf16, i32 = jnp.float32, jnp.bfloat16, jnp.int32


def iota(shape, dim):
    return lax.broadcasted_iota(i32, shape, dim)


def split(v):
    hi = v.astype(bf16)
    return hi, (v - hi.astype(f32)).astype(bf16)


def mm(a, b):
    return jnp.dot(a, b, preferred_element_type=f32)


def kernel(
    amp,
    integ,
    base,
    gap,
    virt,
    amp_ids,
    int_ids,
    res_ids,
    count,
    owners,
    amp_label,
    int_label,
    out,
    pack,
    a_buf,
    ib,
    shi,
    slo,
    tk,
    acc,
    tb,
    near,
    fin,
    a_sem,
    own_sem,
    t_send,
    t_recv,
    x_send,
    x_recv,
    q_send,
    q_recv,
    c_send,
    c_recv,
    n_send,
    n_recv,
    e_send,
    e_recv,
    ok_sem,
):
    g = lax.axis_index("grp")
    w = lax.axis_index("wide")
    x, s = g // 2, g % 2
    z, y = w // 4, w % 4
    par = (y + z) % 2
    right = {"grp": ((x + 1) % 4) * 2 + s, "wide": w}
    left = {"grp": ((x + 3) % 4) * 2 + s, "wide": w}
    twin = {"grp": x * 2 + 1 - s, "wide": w}
    sides = (
        {"grp": g, "wide": z * 4 + (y + 1) % 4},
        {"grp": g, "wide": z * 4 + (y + 3) % 4},
        {"grp": g, "wide": ((z + 1) % 4) * 4 + y},
        {"grp": g, "wide": ((z + 3) % 4) * 4 + y},
    )
    mine = par * 256
    theirs = (1 - par) * 256
    own = g
    along_z = [{"grp": g, "wide": ((z + d) % 4) * 4 + y} for d in range(4)]
    along_y = [{"grp": g, "wide": z * 4 + (y + d) % 4} for d in range(4)]

    def remote(src, dst, send, recv, dev):
        return pltpu.make_async_remote_copy(
            src_ref=src,
            dst_ref=dst,
            send_sem=send,
            recv_sem=recv,
            device_id=dev,
            device_id_type=MESH,
        )

    load = pltpu.make_async_copy(amp, a_buf, a_sem)
    load.start()
    loads = []
    for h in range(2):
        loads.append(
            pltpu.make_async_copy(
                integ.at[0, :, pl.ds(h * 256, 256)], ib.at[h, own], own_sem.at[h]
            )
        )
        loads[h].start()

    pack[...] = jnp.zeros_like(pack)
    used = iota((1, 96), 1) < count[0]
    pack[0:1, 0:96] = jnp.where(used, amp_ids[...], -1)
    pack[1:2, 0:96] = int_ids[...]
    pack[2:3, 0:96] = res_ids[...]

    barrier = pltpu.get_barrier_semaphore()
    for dev in (right, left, twin, *along_z[1:], *along_y[1:]):
        pl.semaphore_signal(barrier, inc=1, device_id=dev, device_id_type=MESH)
    pl.semaphore_wait(barrier, 9)

    for d in range(1, 4):
        pl.semaphore_signal(ok_sem, inc=1, device_id=along_y[d], device_id_type=MESH)

    def task(dz, dy, back=0):
        peer = {"grp": g, "wide": ((z + dz) % 4) * 4 + (y + dy) % 4}
        slot = tb.at[(y - dy) % 4, (z - dz) % 4] if back else tb.at[y, z]
        return remote(pack, slot, t_send.at[dz, dy], t_recv.at[dz, dy], peer)

    beside = [(dz, 0) for dz in (2, 1, 3)] + [(0, dy) for dy in (2, 1, 3)]
    beyond = [(dz, dy) for dz in (2, 1, 3) for dy in (2, 1, 3)]
    for dz, dy in beside:
        task(dz, dy).start()
    keep = pltpu.make_async_copy(pack, tb.at[y, z], t_send.at[0, 0])
    keep.start()

    hop = ((3, 0), (1, 1), (3, 1), (1, 0), (2, 0), (2, 1))

    def block(k, flip=0):
        return 2 * ((x + hop[k][0]) % 4) + (1 - s if flip else s)

    def rows(k, lo=0, n=128):
        return pl.ds(mine + hop[k][1] * 128 + lo, n)

    def x_own(h, k):
        r = rows(k)
        return remote(
            integ.at[0, r, pl.ds(h * 256, 256)],
            ib.at[h, own, r],
            x_send.at[h, k],
            x_recv.at[h, k],
            right if k in (0, 2) else left,
        )

    def x_relay(h, k):
        part = ib.at[h, block(k), rows(k)]
        return remote(
            part, part, x_send.at[h, k + 4], x_recv.at[h, k + 4], right if k == 0 else left
        )

    def x_in(h, k):
        part = ib.at[h, block(k), rows(k)]
        return remote(part, part, x_send.at[h, k], x_recv.at[h, k], right)

    def side_out(h, k, e):
        part = ib.at[h, block(k), rows(k, e * 64, 64)]
        return remote(
            part, part, q_send.at[h, k, e], q_recv.at[h, k, e], sides[hop[k][1] * 2 + e]
        )

    def side_in(h, k, e):
        part = ib.at[h, block(k), pl.ds(theirs + hop[k][1] * 128 + e * 64, 64)]
        return remote(part, part, q_send.at[h, k, e], q_recv.at[h, k, e], right)

    def twin_x(h, k, flip=0):
        part = ib.at[h, block(k, flip), rows(k)]
        return remote(part, part, c_send.at[h, 1 + k], c_recv.at[h, 1 + k], twin)

    first = (0, 1, 4)
    second = (2, 3, 5)

    def twin_q(h, j, flip=0):
        part = ib.at[h, block(first[j], flip), pl.ds(theirs, 256)]
        return remote(part, part, c_send.at[h, 7 + j], c_recv.at[h, 7 + j], twin)

    def twin_own(h):
        return remote(
            integ.at[0, :, pl.ds(h * 256, 256)],
            ib.at[h, own],
            c_send.at[h, 0],
            c_recv.at[h, 0],
            twin,
        )

    def twin_own_in(h):
        part = ib.at[h, 2 * x + 1 - s]
        return remote(part, part, c_send.at[h, 0], c_recv.at[h, 0], twin)

    def got_x(h, k):
        x_in(h, k).wait_recv()
        if k < 2:
            x_relay(h, k).start()
        side_out(h, k, 0).start()
        side_out(h, k, 1).start()
        twin_x(h, k).start()

    def got_q(h, j):
        for k in (first[j], second[j]):
            for e in range(2):
                side_in(h, k, e).wait_recv()
        twin_q(h, j).start()

    def got_twin(h, j):
        twin_x(h, first[j], 1).wait_recv()
        twin_x(h, second[j], 1).wait_recv()
        twin_q(h, j, 1).wait_recv()

    for h, k in ((0, 0), (0, 1), (0, 2), (0, 3), (1, 0), (1, 1)):
        x_own(h, k).start()
    for h in range(2):
        twin_own(h).start()
    pl.semaphore_wait(ok_sem, 3)
    for dz, dy in beyond:
        task(dz, dy).start()

    row = iota((128, 128), 0)

    def column(values, n, which):
        lanes = iota((n, values.shape[1]), 1)
        return jnp.sum(jnp.where(lanes == which, values, 0.0), axis=1, keepdims=True)

    place = iota((128, 1), 0)
    owner = column(owners[...].astype(f32), 128, place % 16).astype(i32)
    sign_c = column((1 - 2 * (int_label[...] & 1)).astype(f32), 128, place // 16)
    sign_b = (1 - 2 * (amp_label[...] & 1)).astype(f32)
    which_c = row // 16
    gaps = column(gap[...], 64, iota((64, 1), 0)).reshape(8, 8, 1)
    local = iota((32, 128), 0) + w * 32
    real = iota((32, 128), 1) < 96

    keep.wait()
    got_x(0, 0)
    got_x(0, 1)
    for k in (2, 3):
        x_own(1, k).start()
    for dz, dy in beside + beyond:
        task(dz, dy, 1).wait_recv()
    hits, picks = [], []
    for v in range(16):
        names = tb[v // 4, v % 4]
        hits.append(
            jnp.where(
                (names[1:2, :] == which_c) & (names[2:3, :] == owner), 1.0, 0.0
            ).astype(bf16)
        )
        picks.append(
            jnp.where((names[0:1, :] == local) & real, 1.0, 0.0).astype(bf16)
        )
    t = lax.dot_general(
        jnp.concatenate(hits, axis=1),
        jnp.concatenate(picks, axis=1),
        (((1,), (1,)), ((), ())),
        preferred_element_type=f32,
    )
    t = (t * sign_b * sign_c).astype(bf16)
    spread = jnp.where(iota((32, 256), 0) == iota((32, 256), 1) // 8, 1.0, 0.0).astype(bf16)
    lift = jnp.where(iota((1024, 128), 1) == iota((1024, 128), 0) // 8, 1.0, 0.0).astype(bf16)
    wide_t = mm(lift, mm(t, spread).astype(bf16))
    tk[...] = jnp.where(
        iota((1024, 256), 0) % 8 == iota((1024, 256), 1) % 8, wide_t, 0.0
    ).astype(bf16)

    load.wait()

    def form(i, _):
        @pl.when(i == 4)
        def _():
            got_x(0, 2)
            got_x(0, 3)

        @pl.when(i == 7)
        def _():
            got_x(1, 0)
            got_x(1, 1)

        part = a_buf[:, pl.ds(pl.multiple_of(i * 8, 8), 8), :].reshape(256, 512)
        hi, lo = split(part)
        both = mm(tk[...], hi) + mm(tk[...], lo)
        hi, lo = split(both)
        shi[:, i] = hi.reshape(8, 128, 512)
        slo[:, i] = lo.reshape(8, 128, 512)
        return 0

    lax.fori_loop(0, 8, form, 0)

    every = pl.ds(0, 4)

    def part(h, a, f, e):
        if a == 0:
            return (h, slice(None), (z + f) % 4, e, slice(None), pl.ds(0, 128))
        return (h, slice(None), e, (y + f) % 4, slice(None), pl.ds(128, 128))

    def first_axis(a):
        return along_y if a else along_z

    def second_axis(a):
        return along_z if a else along_y

    def rs_first(h, a, d):
        return remote(
            acc.at[part(h, a, d, every)],
            near.at[h, a, d],
            n_send.at[h, a, d],
            n_recv.at[h, a, d],
            first_axis(a)[d],
        )

    def rs_last(h, a, d):
        to = (slice(None), ((z if a else y) + d) % 4)
        return remote(
            near.at[(h, a, 0) + to],
            fin.at[h, a, d],
            e_send.at[h, a, d],
            e_recv.at[h, a, d],
            second_axis(a)[d],
        )

    def rs_one(h):
        for d in (2, 1, 3):
            for a in range(2):
                rs_first(h, a, d).start()

    def rs_two(h):
        for a in range(2):
            for d in (1, 3, 2):
                rs_first(h, a, d).wait_recv()
            near[h, a, 0] = (
                near[h, a, 1] + near[h, a, 2] + near[h, a, 3] + acc[part(h, a, 0, every)]
            )
        for d in (2, 1, 3):
            for a in range(2):
                rs_last(h, a, d).start()

    def rs_end(h):
        for a in range(2):
            for d in (1, 3, 2):
                rs_last(h, a, d).wait_recv()
            cols = pl.ds(h * 256 + a * 128, 128)
            out[:, :, cols] = (
                base[:, :, cols]
                + near[h, a, 0, :, z if a else y]
                + fin[h, a, 1]
                + fin[h, a, 2]
                + fin[h, a, 3]
            ) / (gaps + virt[:, cols].reshape(1, 1, 128))

    def events(u):
        if u == 0:
            loads[0].wait()
        if u == 1:
            twin_own_in(0).wait_recv()
            got_x(0, 4)
            got_x(0, 5)
        if u == 2:
            loads[1].wait()
            got_q(0, 0)
            got_q(0, 1)
        if u == 3:
            twin_own_in(1).wait_recv()
            got_x(1, 2)
            got_x(1, 3)
        if u == 5:
            got_q(0, 2)
        if u == 6:
            got_twin(0, 0)
            got_x(1, 4)
            got_x(1, 5)
        if u == 7:
            got_twin(0, 1)
        if u == 8:
            got_q(1, 0)
            got_q(1, 1)
        if u == 9:
            got_twin(0, 2)
        if u == 10:
            rs_one(0)
        if u == 11:
            got_q(1, 2)
        if u == 13:
            got_twin(1, 1)
        if u == 15:
            got_twin(1, 2)
        if u == 12:
            got_twin(1, 0)

    order = [(h, v) for h in range(2) for v in range(2)]
    order += [(h, v) for h in range(2) for v in (2, 4, 3, 5, 6, 7)]
    for u, (h, v) in enumerate(order):
        events(u)
        c = 2 * ((x + (0, 3, 1, 2)[v // 2]) % 4) + (1 - s if v % 2 else s)
        ihi, ilo = split(ib[h, c])
        for r in (slice(0, 4), slice(4, 8)):
            sh = shi[c, r].reshape(512, 512)
            sl = slo[c, r].reshape(512, 512)
            prod = (mm(sh, ihi) + mm(sh, ilo) + mm(sl, ihi)).reshape(4, 4, 4, 8, 256)
            acc[h, r] = prod if v == 0 else acc[h, r] + prod

    rs_one(1)
    rs_two(0)
    rs_two(1)
    rs_end(0)
    rs_end(1)

    for dz, dy in beside + beyond:
        task(dz, dy).wait_send()
    for h in range(2):
        for k in range(4):
            x_own(h, k).wait_send()
        for k in range(2):
            x_relay(h, k).wait_send()
        for k in range(6):
            side_out(h, k, 0).wait_send()
            side_out(h, k, 1).wait_send()
            twin_x(h, k).wait_send()
        for j in range(3):
            twin_q(h, j).wait_send()
        twin_own(h).wait_send()
        for a in range(2):
            for d in (1, 2, 3):
                rs_first(h, a, d).wait_send()
                rs_last(h, a, d).wait_send()


def fused(amplitudes, integrals, base, *small):
    vmem = pl.BlockSpec(memory_space=pltpu.VMEM)
    hbm = pl.BlockSpec(memory_space=pl.ANY)
    smem = pl.BlockSpec(memory_space=pltpu.SMEM)
    dma = pltpu.SemaphoreType.DMA
    return pl.pallas_call(
        kernel,
        out_shape=jax.ShapeDtypeStruct((8, 8, 512), f32),
        in_specs=[hbm, hbm, *[vmem] * 6, smem, *[vmem] * 3],
        out_specs=vmem,
        scratch_shapes=[
            pltpu.VMEM((8, 128), i32),
            pltpu.VMEM((32, 64, 512), f32),
            pltpu.VMEM((2, 8, 512, 256), f32),
            pltpu.VMEM((8, 8, 128, 512), bf16),
            pltpu.VMEM((8, 8, 128, 512), bf16),
            pltpu.VMEM((1024, 256), bf16),
            pltpu.VMEM((2, 8, 4, 4, 8, 256), f32),
            pltpu.VMEM((4, 4, 8, 128), i32),
            pltpu.VMEM((2, 2, 4, 8, 4, 8, 128), f32),
            pltpu.VMEM((2, 2, 4, 8, 8, 128), f32),
            dma,
            dma((2,)),
            dma((4, 4)),
            dma((4, 4)),
            dma((2, 6)),
            dma((2, 6)),
            dma((2, 6, 2)),
            dma((2, 6, 2)),
            dma((2, 10)),
            dma((2, 10)),
            dma((2, 2, 4)),
            dma((2, 2, 4)),
            dma((2, 2, 4)),
            dma((2, 2, 4)),
            pltpu.SemaphoreType.REGULAR,
        ],
        compiler_params=pltpu.CompilerParams(
            collective_id=0, has_side_effects=True, vmem_limit_bytes=60 * 2**20
        ),
    )(amplitudes, integrals, base, *small)


def on_device(
    amplitudes,
    integrals,
    base_residual,
    occ_gap,
    virt_sum,
    task_amp,
    task_int,
    task_res,
    task_count,
    res_owner,
    amp_label,
    int_label,
):
    out = fused(
        amplitudes,
        integrals,
        base_residual.reshape(8, 8, 512),
        occ_gap,
        virt_sum.reshape(1, 512),
        task_amp,
        task_int,
        task_res,
        task_count,
        res_owner,
        amp_label.reshape(1, 32),
        int_label.reshape(1, 8),
    )
    return out.reshape(1, 64, 512)


def solution(mesh):
    both = ("grp", "wide")
    return jax.shard_map(
        on_device,
        mesh=mesh,
        in_specs=(
            P(both, None, None),
            P("grp", None, None),
            P(both, None, None),
            P(both, None),
            P(),
            P(both, None),
            P(both, None),
            P(both, None),
            P(both),
            P("grp", None),
            P(both),
            P(),
        ),
        out_specs=P(both, None, None),
        check_vma=False,
    )
```

```python
import jax
import jax.numpy as jnp
from jax import lax
from jax.experimental import pallas as pl
from jax.experimental.pallas import tpu as pltpu
from jax.sharding import PartitionSpec as P

MESH = pl.DeviceIdType.MESH
f32, bf16, i32 = jnp.float32, jnp.bfloat16, jnp.int32


def iota(shape, dim):
    return lax.broadcasted_iota(i32, shape, dim)


def split(v):
    hi = v.astype(bf16)
    return hi, (v - hi.astype(f32)).astype(bf16)


def mm(a, b):
    return jnp.dot(a, b, preferred_element_type=f32)


def kernel(
    amp,
    integ,
    base,
    gap,
    virt,
    amp_ids,
    int_ids,
    res_ids,
    count,
    owners,
    amp_label,
    int_label,
    out,
    pack,
    a_buf,
    ib,
    shi,
    slo,
    tk,
    acc,
    tb,
    near,
    fin,
    a_sem,
    own_sem,
    t_send,
    t_recv,
    x_send,
    x_recv,
    q_send,
    q_recv,
    c_send,
    c_recv,
    n_send,
    n_recv,
    e_send,
    e_recv,
    ok_sem,
):
    g = lax.axis_index("grp")
    w = lax.axis_index("wide")
    x, s = g // 2, g % 2
    z, y = w // 4, w % 4
    par = (y + z) % 2
    right = {"grp": ((x + 1) % 4) * 2 + s, "wide": w}
    left = {"grp": ((x + 3) % 4) * 2 + s, "wide": w}
    twin = {"grp": x * 2 + 1 - s, "wide": w}
    sides = (
        {"grp": g, "wide": z * 4 + (y + 1) % 4},
        {"grp": g, "wide": z * 4 + (y + 3) % 4},
        {"grp": g, "wide": ((z + 1) % 4) * 4 + y},
        {"grp": g, "wide": ((z + 3) % 4) * 4 + y},
    )
    mine = par * 256
    theirs = (1 - par) * 256
    own = g
    along_z = [{"grp": g, "wide": ((z + d) % 4) * 4 + y} for d in range(4)]
    along_y = [{"grp": g, "wide": z * 4 + (y + d) % 4} for d in range(4)]

    def remote(src, dst, send, recv, dev):
        return pltpu.make_async_remote_copy(
            src_ref=src,
            dst_ref=dst,
            send_sem=send,
            recv_sem=recv,
            device_id=dev,
            device_id_type=MESH,
        )

    barrier = pltpu.get_barrier_semaphore()
    for dev in (right, left, twin, *along_z[1:], *along_y[1:]):
        pl.semaphore_signal(barrier, inc=1, device_id=dev, device_id_type=MESH)
    load = pltpu.make_async_copy(amp, a_buf, a_sem)
    load.start()
    loads = []
    for h in range(2):
        loads.append(
            pltpu.make_async_copy(
                integ.at[0, :, pl.ds(h * 256, 256)], ib.at[h, own], own_sem.at[h]
            )
        )
        loads[h].start()

    pack[...] = jnp.zeros_like(pack)
    used = iota((1, 96), 1) < count[0]
    pack[0:1, 0:96] = jnp.where(used, amp_ids[...], -1)
    pack[1:2, 0:96] = int_ids[...]
    pack[2:3, 0:96] = res_ids[...]
    pl.semaphore_wait(barrier, 9)

    for d in range(1, 4):
        pl.semaphore_signal(ok_sem, inc=1, device_id=along_y[d], device_id_type=MESH)

    def task(dz, dy, back=0):
        peer = {"grp": g, "wide": ((z + dz) % 4) * 4 + (y + dy) % 4}
        slot = tb.at[(y - dy) % 4, (z - dz) % 4] if back else tb.at[y, z]
        return remote(pack, slot, t_send.at[dz, dy], t_recv.at[dz, dy], peer)

    beside = [(dz, 0) for dz in (2, 1, 3)] + [(0, dy) for dy in (2, 1, 3)]
    beyond = [(dz, dy) for dz in (2, 1, 3) for dy in (2, 1, 3)]
    for dz, dy in beside:
        task(dz, dy).start()
    keep = pltpu.make_async_copy(pack, tb.at[y, z], t_send.at[0, 0])
    keep.start()

    hop = ((3, 0), (1, 1), (3, 1), (1, 0), (2, 0), (2, 1))

    def block(k, flip=0):
        return 2 * ((x + hop[k][0]) % 4) + (1 - s if flip else s)

    def rows(k, lo=0, n=128):
        return pl.ds(mine + hop[k][1] * 128 + lo, n)

    def x_own(h, k):
        r = rows(k)
        return remote(
            integ.at[0, r, pl.ds(h * 256, 256)],
            ib.at[h, own, r],
            x_send.at[h, k],
            x_recv.at[h, k],
            right if k in (0, 2) else left,
        )

    def x_relay(h, k):
        part = ib.at[h, block(k), rows(k)]
        return remote(
            part, part, x_send.at[h, k + 4], x_recv.at[h, k + 4], right if k == 0 else left
        )

    def x_in(h, k):
        part = ib.at[h, block(k), rows(k)]
        return remote(part, part, x_send.at[h, k], x_recv.at[h, k], right)

    def side_out(h, k, e):
        part = ib.at[h, block(k), rows(k, e * 64, 64)]
        return remote(
            part, part, q_send.at[h, k, e], q_recv.at[h, k, e], sides[hop[k][1] * 2 + e]
        )

    def side_in(h, k, e):
        part = ib.at[h, block(k), pl.ds(theirs + hop[k][1] * 128 + e * 64, 64)]
        return remote(part, part, q_send.at[h, k, e], q_recv.at[h, k, e], right)

    def twin_x(h, k, flip=0):
        part = ib.at[h, block(k, flip), rows(k)]
        return remote(part, part, c_send.at[h, 1 + k], c_recv.at[h, 1 + k], twin)

    first = (0, 1, 4)
    second = (2, 3, 5)

    def twin_q(h, j, flip=0):
        part = ib.at[h, block(first[j], flip), pl.ds(theirs, 256)]
        return remote(part, part, c_send.at[h, 7 + j], c_recv.at[h, 7 + j], twin)

    def twin_own(h):
        return remote(
            integ.at[0, :, pl.ds(h * 256, 256)],
            ib.at[h, own],
            c_send.at[h, 0],
            c_recv.at[h, 0],
            twin,
        )

    def twin_own_in(h):
        part = ib.at[h, 2 * x + 1 - s]
        return remote(part, part, c_send.at[h, 0], c_recv.at[h, 0], twin)

    def got_x(h, k):
        x_in(h, k).wait_recv()
        if k < 2:
            x_relay(h, k).start()
        side_out(h, k, 0).start()
        side_out(h, k, 1).start()
        twin_x(h, k).start()

    def got_q(h, j):
        for k in (first[j], second[j]):
            for e in range(2):
                side_in(h, k, e).wait_recv()
        twin_q(h, j).start()

    def got_twin(h, j):
        twin_x(h, first[j], 1).wait_recv()
        twin_x(h, second[j], 1).wait_recv()
        twin_q(h, j, 1).wait_recv()

    for h, k in ((0, 0), (0, 1), (0, 2), (0, 3), (1, 0), (1, 1)):
        x_own(h, k).start()
    for h in range(2):
        twin_own(h).start()
    pl.semaphore_wait(ok_sem, 3)
    for dz, dy in beyond:
        task(dz, dy).start()

    row = iota((128, 128), 0)

    def column(values, n, which):
        lanes = iota((n, values.shape[1]), 1)
        return jnp.sum(jnp.where(lanes == which, values, 0.0), axis=1, keepdims=True)

    place = iota((128, 1), 0)
    owner = column(owners[...].astype(f32), 128, place % 16).astype(i32)
    sign_c = column((1 - 2 * (int_label[...] & 1)).astype(f32), 128, place // 16)
    sign_b = (1 - 2 * (amp_label[...] & 1)).astype(f32)
    which_c = row // 16
    gaps = column(gap[...], 64, iota((64, 1), 0)).reshape(8, 8, 1)
    local = iota((32, 128), 0) + w * 32
    real = iota((32, 128), 1) < 96

    keep.wait()
    for dz, dy in beside + beyond:
        task(dz, dy, 1).wait_recv()
    got_x(0, 0)
    got_x(0, 1)
    for k in (2, 3):
        x_own(1, k).start()
    hits, picks = [], []
    for v in range(16):
        names = tb[v // 4, v % 4]
        hits.append(
            jnp.where(
                (names[1:2, :] == which_c) & (names[2:3, :] == owner), 1.0, 0.0
            ).astype(bf16)
        )
        picks.append(
            jnp.where((names[0:1, :] == local) & real, 1.0, 0.0).astype(bf16)
        )
    t = lax.dot_general(
        jnp.concatenate(hits, axis=1),
        jnp.concatenate(picks, axis=1),
        (((1,), (1,)), ((), ())),
        preferred_element_type=f32,
    )
    t = (t * sign_b * sign_c).astype(bf16)
    spread = jnp.where(iota((32, 256), 0) == iota((32, 256), 1) // 8, 1.0, 0.0).astype(bf16)
    lift = jnp.where(iota((1024, 128), 1) == iota((1024, 128), 0) // 8, 1.0, 0.0).astype(bf16)
    wide_t = mm(lift, mm(t, spread).astype(bf16))
    tk[...] = jnp.where(
        iota((1024, 256), 0) % 8 == iota((1024, 256), 1) % 8, wide_t, 0.0
    ).astype(bf16)

    load.wait()

    def form(i, _):
        @pl.when(i == 4)
        def _():
            got_x(0, 2)
            got_x(0, 3)

        @pl.when(i == 7)
        def _():
            got_x(1, 0)
            got_x(1, 1)

        part = a_buf[:, pl.ds(pl.multiple_of(i * 8, 8), 8), :].reshape(256, 512)
        hi, lo = split(part)
        both = mm(tk[...], hi) + mm(tk[...], lo)
        hi, lo = split(both)
        shi[:, i] = hi.reshape(8, 128, 512)
        slo[:, i] = lo.reshape(8, 128, 512)
        return 0

    lax.fori_loop(0, 8, form, 0)

    every = pl.ds(0, 4)

    def part(h, a, f, e):
        if a == 0:
            return (h, slice(None), (z + f) % 4, e, slice(None), pl.ds(0, 128))
        return (h, slice(None), e, (y + f) % 4, slice(None), pl.ds(128, 128))

    def first_axis(a):
        return along_y if a else along_z

    def second_axis(a):
        return along_z if a else along_y

    def rs_first(h, a, d):
        return remote(
            acc.at[part(h, a, d, every)],
            near.at[h, a, d],
            n_send.at[h, a, d],
            n_recv.at[h, a, d],
            first_axis(a)[d],
        )

    def rs_last(h, a, d):
        to = (slice(None), ((z if a else y) + d) % 4)
        return remote(
            near.at[(h, a, 0) + to],
            fin.at[h, a, d],
            e_send.at[h, a, d],
            e_recv.at[h, a, d],
            second_axis(a)[d],
        )

    def rs_one(h):
        for d in (2, 1, 3):
            for a in range(2):
                rs_first(h, a, d).start()

    def rs_two(h):
        for a in range(2):
            for d in (1, 3, 2):
                rs_first(h, a, d).wait_recv()
            near[h, a, 0] = (
                near[h, a, 1] + near[h, a, 2] + near[h, a, 3] + acc[part(h, a, 0, every)]
            )
        for d in (2, 1, 3):
            for a in range(2):
                rs_last(h, a, d).start()

    def rs_end(h):
        for a in range(2):
            for d in (1, 3, 2):
                rs_last(h, a, d).wait_recv()
            cols = pl.ds(h * 256 + a * 128, 128)
            out[:, :, cols] = (
                base[:, :, cols]
                + near[h, a, 0, :, z if a else y]
                + fin[h, a, 1]
                + fin[h, a, 2]
                + fin[h, a, 3]
            ) / (gaps + virt[:, cols].reshape(1, 1, 128))

    def events(u):
        if u == 0:
            loads[0].wait()
        if u == 1:
            twin_own_in(0).wait_recv()
            got_x(0, 4)
            got_x(0, 5)
        if u == 2:
            loads[1].wait()
            got_q(0, 0)
            got_q(0, 1)
        if u == 3:
            twin_own_in(1).wait_recv()
            got_x(1, 2)
            got_x(1, 3)
        if u == 5:
            got_q(0, 2)
        if u == 6:
            got_twin(0, 0)
            got_x(1, 4)
            got_x(1, 5)
        if u == 7:
            got_twin(0, 1)
        if u == 8:
            got_q(1, 0)
            got_q(1, 1)
        if u == 9:
            got_twin(0, 2)
        if u == 10:
            rs_one(0)
        if u == 11:
            got_q(1, 2)
        if u == 13:
            got_twin(1, 1)
        if u == 15:
            got_twin(1, 2)
        if u == 12:
            got_twin(1, 0)

    order = [(h, v) for h in range(2) for v in range(2)]
    order += [(h, v) for h in range(2) for v in (2, 4, 3, 5, 6, 7)]
    for u, (h, v) in enumerate(order):
        events(u)
        c = 2 * ((x + (0, 3, 1, 2)[v // 2]) % 4) + (1 - s if v % 2 else s)
        ihi, ilo = split(ib[h, c])
        for r in (slice(0, 4), slice(4, 8)):
            sh = shi[c, r].reshape(512, 512)
            sl = slo[c, r].reshape(512, 512)
            prod = (mm(sh, ihi) + mm(sh, ilo) + mm(sl, ihi)).reshape(4, 4, 4, 8, 256)
            acc[h, r] = prod if v == 0 else acc[h, r] + prod

    rs_one(1)
    rs_two(0)
    rs_two(1)
    rs_end(0)
    rs_end(1)

    for dz, dy in beside + beyond:
        task(dz, dy).wait_send()
    for h in range(2):
        for k in range(4):
            x_own(h, k).wait_send()
        for k in range(2):
            x_relay(h, k).wait_send()
        for k in range(6):
            side_out(h, k, 0).wait_send()
            side_out(h, k, 1).wait_send()
            twin_x(h, k).wait_send()
        for j in range(3):
            twin_q(h, j).wait_send()
        twin_own(h).wait_send()
        for a in range(2):
            for d in (1, 2, 3):
                rs_first(h, a, d).wait_send()
                rs_last(h, a, d).wait_send()


def fused(amplitudes, integrals, base, *small):
    vmem = pl.BlockSpec(memory_space=pltpu.VMEM)
    hbm = pl.BlockSpec(memory_space=pl.ANY)
    smem = pl.BlockSpec(memory_space=pltpu.SMEM)
    dma = pltpu.SemaphoreType.DMA
    return pl.pallas_call(
        kernel,
        out_shape=jax.ShapeDtypeStruct((8, 8, 512), f32),
        in_specs=[hbm, hbm, *[vmem] * 6, smem, *[vmem] * 3],
        out_specs=vmem,
        scratch_shapes=[
            pltpu.VMEM((8, 128), i32),
            pltpu.VMEM((32, 64, 512), f32),
            pltpu.VMEM((2, 8, 512, 256), f32),
            pltpu.VMEM((8, 8, 128, 512), bf16),
            pltpu.VMEM((8, 8, 128, 512), bf16),
            pltpu.VMEM((1024, 256), bf16),
            pltpu.VMEM((2, 8, 4, 4, 8, 256), f32),
            pltpu.VMEM((4, 4, 8, 128), i32),
            pltpu.VMEM((2, 2, 4, 8, 4, 8, 128), f32),
            pltpu.VMEM((2, 2, 4, 8, 8, 128), f32),
            dma,
            dma((2,)),
            dma((4, 4)),
            dma((4, 4)),
            dma((2, 6)),
            dma((2, 6)),
            dma((2, 6, 2)),
            dma((2, 6, 2)),
            dma((2, 10)),
            dma((2, 10)),
            dma((2, 2, 4)),
            dma((2, 2, 4)),
            dma((2, 2, 4)),
            dma((2, 2, 4)),
            pltpu.SemaphoreType.REGULAR,
        ],
        compiler_params=pltpu.CompilerParams(
            collective_id=0, has_side_effects=True, vmem_limit_bytes=60 * 2**20
        ),
    )(amplitudes, integrals, base, *small)


def on_device(
    amplitudes,
    integrals,
    base_residual,
    occ_gap,
    virt_sum,
    task_amp,
    task_int,
    task_res,
    task_count,
    res_owner,
    amp_label,
    int_label,
):
    out = fused(
        amplitudes,
        integrals,
        base_residual.reshape(8, 8, 512),
        occ_gap,
        virt_sum.reshape(1, 512),
        task_amp,
        task_int,
        task_res,
        task_count,
        res_owner,
        amp_label.reshape(1, 32),
        int_label.reshape(1, 8),
    )
    return out.reshape(1, 64, 512)


def solution(mesh):
    both = ("grp", "wide")
    return jax.shard_map(
        on_device,
        mesh=mesh,
        in_specs=(
            P(both, None, None),
            P("grp", None, None),
            P(both, None, None),
            P(both, None),
            P(),
            P(both, None),
            P(both, None),
            P(both, None),
            P(both),
            P("grp", None),
            P(both),
            P(),
        ),
        out_specs=P(both, None, None),
        check_vma=False,
    )
```
